512 devices in a mesh: depth: 8 (over x, core), sx: 8 (over z), sy: 8 (over y).
Axes of the slice: x: 4, y: 8, z: 8, core: 2. Of those that a mesh axis runs over, the one named last changes fastest.
Arguments:
- transmission: bfloat16 [16, 2, 2048, 2048], P('depth', None, 'sx', 'sy')
- incident: bfloat16 [16, 128, 2, 256, 256], P('depth', ('sx', 'sy')), may hold values from -6 to 6
- exit_adjoint: bfloat16 [128, 2, 256, 256], P(('sx', 'sy')), may hold values from -6 to 6
- propagator_phase: float32 [256, 256], replicated, may hold values from -3.140625 to 3.140625
- scan_anchor: int32 [128, 2], P(('sx', 'sy')), may hold values from -128 to 1919, as said below
- live_count: int32 [64], P(('sx', 'sy')), may hold values from 1 to 2, as said below
Outputs:
- gradient: float32 [16, 2, 2048, 2048], P('depth', None, 'sx', 'sy')
The draws below stay inside these ranges and needn't reach their ends.
Inputs may be any that keep to these rules, and one draw needn't show every extreme that they name: `scan_anchor`: the slot at position p of the device at indices (a, b) of (sx, sy), slot a * 2 * 8 + b * 2 + p, has its x anchor in [a * 256 - 256 // 2, a * 256 + 256 - 256 // 2) and its y anchor in [b * 256 - 256 // 2, b * 256 + 256 - 256 // 2). Both ends of the whole range are taken in every draw. The live slots of a device are its first live_count slots; some device has all 2 slots live and some device exactly one.
All inputs are finite; a program needn't handle non-finite values.
Results may differ from the reference program's by a relative error of at most 0.0003.
Values may be sent and summed in bfloat16 or wider, within the bound.
A program may use at most 128 MiB of HBM per device.

```python
import math
import jax
import jax.numpy as jnp
from jax import lax

PATCH = 256
TILE = 256
P_DEV = 2
SLICES = 16
NX = 2048
NY = 2048
SCANS = 128


def draw_transmission(key, part):
    key_amp, key_phase = jax.random.split(jax.random.fold_in(key, 11))
    amplitude = jax.random.uniform(key_amp, (SLICES, NX, NY), jnp.float32, 0.9, 1.0)
    phase = jax.random.uniform(key_phase, (SLICES, NX, NY), jnp.float32, -math.pi, math.pi)
    return jnp.stack([amplitude * jnp.cos(phase), amplitude * jnp.sin(phase)], axis=1).astype(jnp.bfloat16)


def draw_scan_anchor(key, part):
    keys = jax.random.split(jax.random.fold_in(key, 23), 10)
    tiles_x = NX // TILE
    tiles_y = NY // TILE
    half = PATCH // 2
    slot_ids = jnp.arange(SCANS, dtype=jnp.int32)
    device = slot_ids // P_DEV
    tile_x = device // tiles_y
    tile_y = device % tiles_y
    within_x = jax.random.randint(keys[0], (SCANS,), 0, TILE, jnp.int32)
    within_y = jax.random.randint(keys[1], (SCANS,), 0, TILE, jnp.int32)
    low_x = jax.random.randint(keys[2], (), 0, tiles_y, jnp.int32) * P_DEV + jax.random.randint(keys[3], (), 0, P_DEV, jnp.int32)
    high_x = ((tiles_x - 1) * tiles_y + jax.random.randint(keys[4], (), 0, tiles_y, jnp.int32)) * P_DEV + jax.random.randint(keys[5], (), 0, P_DEV, jnp.int32)
    low_y = jax.random.randint(keys[6], (), 0, tiles_x, jnp.int32) * tiles_y * P_DEV + jax.random.randint(keys[7], (), 0, P_DEV, jnp.int32)
    high_y = (jax.random.randint(keys[8], (), 0, tiles_x, jnp.int32) * tiles_y + tiles_y - 1) * P_DEV + jax.random.randint(keys[9], (), 0, P_DEV, jnp.int32)
    within_x = within_x.at[low_x].set(0).at[high_x].set(TILE - 1)
    within_y = within_y.at[low_y].set(0).at[high_y].set(TILE - 1)
    anchor_x = tile_x * TILE - half + within_x
    anchor_y = tile_y * TILE - half + within_y
    return jnp.stack([anchor_x, anchor_y], axis=1).astype(jnp.int32)


def draw_live_count(key, part):
    devices = SCANS // P_DEV
    key_level, key_full = jax.random.split(jax.random.fold_in(key, 37))
    level = jax.random.randint(key_level, (devices,), 0, 5, jnp.int32)
    counts = jnp.where(level < 3, 1, jnp.where(level == 3, max(1, P_DEV // 2), P_DEV)).astype(jnp.int32)
    busiest = jax.random.randint(key_full, (), 0, devices, jnp.int32)
    counts = counts.at[busiest].set(P_DEV)
    counts = counts.at[(busiest + 1) % devices].set(1)
    return counts.astype(jnp.int32)


def block_scale(key, dims, shards, low, top_value):
    def one(dim, shards_of):
        heights = jax.random.uniform(jax.random.fold_in(jax.random.fold_in(key, 6), dim), (shards_of,), jnp.float32, low / len(shards), top_value / len(shards))
        return jnp.repeat(jnp.exp(heights), dims[dim] // shards_of).reshape((-1,) + (1,) * (len(dims) - dim - 1))

    loudness = one(*shards[0])
    for cut in shards[1:]:
        loudness = loudness * one(*cut)
    return loudness


def bell_draw(own_key, dims, scale, reach, pieces=(), held_as=jnp.bfloat16):
    array = scale * jax.random.normal(own_key, dims, jnp.float32)
    if pieces:
        array = array * block_scale(own_key, dims, pieces, -0.22, 0.18)
    return jnp.clip(array, -reach, reach).astype(held_as)


def setup_inputs(seed: int = 0) -> dict:
    key_list = jax.random.split(jax.random.key(seed), 7)
    transmission = draw_transmission(jax.random.fold_in(key_list[6], 71), 0)
    incident = bell_draw(key_list[1], (SLICES, SCANS, 2, PATCH, PATCH), 1.0, 6.0, ((0, 8), (1, 64)))
    exit_adjoint = bell_draw(key_list[2], (SCANS, 2, PATCH, PATCH), 1.0, 6.0, ((0, 64),))
    propagator_phase = jnp.clip(jax.random.uniform(key_list[3], (PATCH, PATCH), jnp.float32, -3.140625, 3.140625), -3.140625, 3.140625)
    scan_anchor = draw_scan_anchor(jax.random.fold_in(key_list[6], 71), 0)
    live_count = draw_live_count(jax.random.fold_in(key_list[6], 71), 0)
    return dict(transmission=transmission, incident=incident, exit_adjoint=exit_adjoint, propagator_phase=propagator_phase, scan_anchor=scan_anchor, live_count=live_count)


def reference(transmission, incident, exit_adjoint, propagator_phase, scan_anchor, live_count):
    half = PATCH // 2
    padded = jnp.pad(transmission.astype(jnp.float32), ((0, 0), (0, 0), (half, half), (half, half)))
    object_field = lax.complex(padded[:, 0], padded[:, 1])
    phase = propagator_phase.astype(jnp.float32)
    rotation = lax.complex(jnp.cos(phase), -jnp.sin(phase))
    slot_ids = jnp.arange(SCANS, dtype=jnp.int32)
    live = (slot_ids % P_DEV < live_count[slot_ids // P_DEV]).astype(jnp.float32)
    start_field = jnp.zeros(object_field.shape, object_field.dtype)

    def one_slot(slot, accumulated):
        corner_x = (scan_anchor[slot, 0] + half).astype(jnp.int32)
        corner_y = (scan_anchor[slot, 1] + half).astype(jnp.int32)
        wave = lax.complex(exit_adjoint[slot, 0].astype(jnp.float32), exit_adjoint[slot, 1].astype(jnp.float32)) * live[slot]
        for layer in range(SLICES - 1, -1, -1):
            start = (jnp.asarray(layer, jnp.int32), corner_x, corner_y)
            entering = lax.complex(incident[layer, slot, 0].astype(jnp.float32), incident[layer, slot, 1].astype(jnp.float32))
            current = lax.dynamic_slice(accumulated, start, (1, PATCH, PATCH))
            accumulated = lax.dynamic_update_slice(accumulated, current + (jnp.conj(entering) * wave)[None], start)
            window = lax.dynamic_slice(object_field, start, (1, PATCH, PATCH))[0]
            wave = jnp.conj(window) * wave
            if layer > 0:
                wave = jnp.fft.ifft2(jnp.fft.fft2(wave, norm="ortho") * rotation, norm="ortho")
        return accumulated

    accumulated = lax.fori_loop(0, SCANS, one_slot, start_field)
    inner = accumulated[:, half:half + NX, half:half + NY]
    return jnp.stack([jnp.real(inner), jnp.imag(inner)], axis=1).astype(jnp.float32)
```

```python
import functools

import ml_dtypes
import numpy as np
import jax
import jax.numpy as jnp
from jax import lax
from jax.experimental import pallas as pl
from jax.experimental.pallas import tpu as pltpu
from jax.sharding import PartitionSpec as P

TILE = 256
HALF = 128
MESH = pl.DeviceIdType.MESH
F32 = jnp.float32
BF16 = jnp.bfloat16


def dft_tables():
    n = np.arange(HALF)
    angle = 2.0 * np.pi * ((n[:, None] * n[None, :]) % HALF) / HALF
    c, s = np.cos(angle) / 16.0, np.sin(angle) / 16.0
    m = np.block([[c, s], [-s, c]])
    out = []
    for a in (m, m.T):
        head = a.astype(ml_dtypes.bfloat16)
        out += [head, (a - head.astype(np.float64)).astype(ml_dtypes.bfloat16)]
    return np.stack(out)


def twiddles():
    n = 2.0 * np.pi * np.arange(HALF) / TILE
    rows = np.stack([np.cos(n), np.sin(n)])
    return (
        np.broadcast_to(rows[:, :, None], (2, HALF, HALF)).astype(np.float32),
        np.broadcast_to(rows[:, None, :], (2, 8, HALF)).astype(np.float32),
    )


def halves(x):
    head = x.astype(BF16)
    return head, (x - head.astype(F32)).astype(BF16)


def conj_times(ar, ai, br, bi):
    return ar * br + ai * bi, ar * bi - ai * br


def dot(a, b):
    return jnp.dot(a, b, preferred_element_type=F32)


def kernel(
    sizes,
    t_hbm,
    inc_hbm,
    exit_hbm,
    phase_hbm,
    m_hbm,
    rows_hbm,
    lane_ref,
    anchor_ref,
    live_ref,
    out_hbm,
    t_own,
    t_alt,
    t_eff,
    inc,
    exit_v,
    phase,
    rot,
    m_v,
    rows_v,
    waves,
    middle,
    sent,
    zbuf,
    ebuf,
    g_own,
    g_alt,
    g_in,
    load_sem,
    t_send,
    t_recv,
    w_send,
    w_recv,
    g_send,
    g_recv,
    out_sem,
):
    n_depth, n_sx, n_sy = sizes
    d, sx, sy = lax.axis_index("depth"), lax.axis_index("sx"), lax.axis_index("sy")
    last = n_depth - 1

    def at(dx, dy):
        return (d, lax.rem(sx + dx + n_sx, n_sx), lax.rem(sy + dy + n_sy, n_sy))

    around = [(i, j) for i in (-1, 0, 1) for j in (-1, 0, 1) if (i, j) != (0, 0)]

    loads = [
        pltpu.make_async_copy(src, dst, load_sem.at[i])
        for i, (src, dst) in enumerate(
            [
                (phase_hbm, phase),
                (m_hbm, m_v),
                (rows_hbm, rows_v),
                (exit_hbm, exit_v),
                (inc_hbm, inc),
                (t_hbm, t_own),
            ]
        )
    ]
    for c in loads:
        c.start()

    barrier = pltpu.get_barrier_semaphore()
    for i, j in around:
        pl.semaphore_signal(barrier, inc=1, device_id=at(i, j), device_id_type=MESH)

    for step in (1, last):
        near = (lax.rem(d + step, n_depth), sx, sy)
        pl.semaphore_signal(barrier, inc=1, device_id=near, device_id_type=MESH)
    pl.semaphore_wait(barrier, len(around) + 2)

    full = pl.ds(0, TILE)
    part = [pl.ds(0, HALF), pl.ds(HALF, HALF)]
    toward = [-1, 1]
    pieces = (
        [(0, part[p], full, (toward[p], 0)) for p in (0, 1)]
        + [(1, full, part[q], (0, toward[q])) for q in (0, 1)]
        + [(2, part[p], part[q], (toward[p], toward[q])) for p in (0, 1) for q in (0, 1)]
    )

    def t_copies(li):
        return [
            pltpu.make_async_remote_copy(
                src_ref=t_hbm.at[li, :, rows, lanes],
                dst_ref=t_alt.at[li, kind, :, rows, lanes],
                send_sem=t_send.at[li * 8 + i],
                recv_sem=t_recv.at[li * 8 + i],
                device_id=at(*way),
                device_id_type=MESH,
            )
            for i, (kind, rows, lanes, way) in enumerate(pieces)
        ]

    def g_copies(li):
        return [
            pltpu.make_async_remote_copy(
                src_ref=g_alt.at[li, kind, :, rows, lanes],
                dst_ref=g_in.at[li, kind, :, rows, lanes],
                send_sem=g_send.at[li * 8 + i],
                recv_sem=g_recv.at[li * 8 + i],
                device_id=at(-way[0], -way[1]),
                device_id_type=MESH,
            )
            for i, (kind, rows, lanes, way) in enumerate(pieces)
        ]

    def w_copy(slot, h):
        return pltpu.make_async_remote_copy(
            src_ref=sent.at[slot, h],
            dst_ref=waves.at[slot, h],
            send_sem=w_send.at[slot * 2 + h],
            recv_sem=w_recv.at[slot * 2 + h],
            device_id=(lax.rem(d + last, n_depth), sx, sy),
            device_id_type=MESH,
        )

    for li in (1, 0):
        for c in t_copies(li):
            c.start()

    def offsets(slot):
        return anchor_ref[slot, 0] - sx * TILE, anchor_ref[slot, 1] - sy * TILE

    def spans(slot):
        ax, ay = offsets(slot)
        out = []
        for a, k, n in ((ax, sx, n_sx), (ay, sy, n_sy)):
            low, high = jnp.maximum(a, 0), TILE + jnp.minimum(a, 0)
            out.append((low, high, jnp.where(k < n - 1, low, 0), jnp.where(k > 0, high, TILE)))
        return out

    def masks(slot, h):
        (lx, hx, olx, ohx), (ly, hy, oly, ohy) = spans(slot)
        r = lax.broadcasted_iota(jnp.int32, (HALF, TILE), 0) + h * HALF
        c = lax.broadcasted_iota(jnp.int32, (HALF, TILE), 1)
        own_x = (r >= lx) & (r < hx)
        own_y = (c >= ly) & (c < hy)
        alt_x = (r < olx) | (r >= ohx)
        alt_y = (c < oly) | (c >= ohy)
        return own_x, own_y, alt_x, alt_y

    def rolled(slot, fields):
        ax, ay = offsets(slot)
        i = lax.broadcasted_iota(jnp.int32, (TILE, TILE), 0)
        j = lax.broadcasted_iota(jnp.int32, (TILE, TILE), 1)
        by_rows = jnp.where(((j + ax - i) & (TILE - 1)) == 0, 1.0, 0.0).astype(BF16)
        by_lanes = jnp.where(((i + ay - j) & (TILE - 1)) == 0, 1.0, 0.0).astype(BF16)
        return [dot(by_rows, dot(f, by_lanes).astype(BF16)) for f in fields]

    for c in loads[:5]:
        c.wait()

    @pl.when(d == last)
    def _():
        for slot in (0, 1):
            alive = jnp.where(slot < live_ref[0], 1.0, 0.0).astype(F32)
            for k, f in enumerate(rolled(slot, [exit_v[slot, 0], exit_v[slot, 1]])):
                for h in (0, 1):
                    waves[slot, h, k] = f[h * HALF : (h + 1) * HALF] * alive

    i = lax.broadcasted_iota(jnp.int32, (TILE, TILE), 0)
    j = lax.broadcasted_iota(jnp.int32, (TILE, TILE), 1)
    deal = jnp.where(i == jnp.where(j < HALF, 2 * j, 2 * j - (TILE - 1)), 1.0, 0.0).astype(BF16)
    deal_rows = jnp.where(j == jnp.where(i < HALF, 2 * i, 2 * i - (TILE - 1)), 1.0, 0.0).astype(BF16)
    p = phase[...]
    p0 = p.astype(BF16)
    p1, p2 = halves(p - p0.astype(F32))
    f0, f1, f2 = [dot(deal_rows, dot(q, deal).astype(BF16)) for q in (p0, p1, p2)]
    phase[...] = (f0 + f1) + f2
    for h in (0, 1):
        ordered = phase[part[h], :]
        rot[0, h] = jnp.cos(ordered)
        rot[1, h] = jnp.sin(ordered)

    def roll_incident(slot):
        got = rolled(slot, [inc[li, slot, k] for li in (0, 1) for k in (0, 1)])
        for n, f in enumerate(got):
            inc[n // 2, slot, n % 2] = f.astype(BF16)

    for slot in (0, 1):
        roll_incident(slot)

    zero = jnp.zeros((HALF, TILE), F32)

    def window(li, slot):
        for h in (0, 1):
            own_x, own_y, alt_x, alt_y = masks(slot, h)
            rows = part[h]
            for k in (0, 1):
                here = t_own[li, k, rows, :].astype(F32)
                tx = t_alt[li, 0, k, rows, :].astype(F32)
                ty = t_alt[li, 1, k, rows, :].astype(F32)
                txy = t_alt[li, 2, k, rows, :].astype(F32)
                inner = jnp.where(own_y, here, jnp.where(alt_y, ty, zero))
                outer = jnp.where(own_y, tx, jnp.where(alt_y, txy, zero))
                t_eff[li, slot, k, rows, :] = jnp.where(
                    own_x, inner, jnp.where(alt_x, outer, zero)
                ).astype(BF16)

    cl, sl = lane_ref[0, 0:1, :], lane_ref[1, 0:1, :]

    def right(z, first):
        head, tail = halves(z)
        table = jnp.concatenate([m_v[first], m_v[first], m_v[first + 1]], axis=0)
        return dot(jnp.concatenate([head, tail, head], axis=1), table)

    def left(z, first):
        head, tail = halves(z)
        table = jnp.concatenate([m_v[first], m_v[first + 1], m_v[first]], axis=1)
        return dot(table, jnp.concatenate([head, head, tail], axis=0))

    def right_forward(h, re, im):
        sr, dr = re[:, :HALF] + re[:, HALF:], re[:, :HALF] - re[:, HALF:]
        si, di = im[:, :HALF] + im[:, HALF:], im[:, :HALF] - im[:, HALF:]
        tr, ti = dr * cl + di * sl, di * cl - dr * sl
        z = jnp.concatenate(
            [jnp.concatenate([sr, si], axis=1), jnp.concatenate([tr, ti], axis=1)], axis=0
        )
        y = right(z, 2)
        zbuf[h, 0, :, :HALF] = y[:HALF, :HALF]
        zbuf[h, 0, :, HALF:] = y[HALF:, :HALF]
        zbuf[h, 1, :, :HALF] = y[:HALF, HALF:]
        zbuf[h, 1, :, HALF:] = y[HALF:, HALF:]

    def row_twiddle():
        c, s = rows_v[0], rows_v[1]
        return jnp.concatenate([c, c], axis=1), jnp.concatenate([s, s], axis=1)

    def spectrum():
        for h in (0, 1):
            if h == 0:
                zr, zi = zbuf[0, 0] + zbuf[1, 0], zbuf[0, 1] + zbuf[1, 1]
            else:
                c, s = row_twiddle()
                dr, di = zbuf[0, 0] - zbuf[1, 0], zbuf[0, 1] - zbuf[1, 1]
                zr, zi = dr * c + di * s, di * c - dr * s
            x = left(jnp.concatenate([zr, zi], axis=0), 0)
            xr, xi = x[:HALF], x[HALF:]
            cp, sp = rot[0, h], rot[1, h]
            y = jnp.concatenate([xr * cp + xi * sp, xi * cp - xr * sp], axis=0)
            e = left(y, 2)
            er, ei = e[:HALF], e[HALF:]
            if h == 1:
                er, ei = er * c - ei * s, ei * c + er * s
            ebuf[h, 0] = er
            ebuf[h, 1] = ei

    def right_inverse(h, store):
        if h == 0:
            vr, vi = ebuf[0, 0] + ebuf[1, 0], ebuf[0, 1] + ebuf[1, 1]
        else:
            vr, vi = ebuf[0, 0] - ebuf[1, 0], ebuf[0, 1] - ebuf[1, 1]
        z = jnp.concatenate(
            [
                jnp.concatenate([vr[:, :HALF], vi[:, :HALF]], axis=1),
                jnp.concatenate([vr[:, HALF:], vi[:, HALF:]], axis=1),
            ],
            axis=0,
        )
        y = right(z, 0)
        er, ei, orr, oi = y[:HALF, :HALF], y[:HALF, HALF:], y[HALF:, :HALF], y[HALF:, HALF:]
        tr, ti = orr * cl - oi * sl, oi * cl + orr * sl
        store(0, er + tr, er - tr)
        store(1, ei + ti, ei - ti)

    def through(li, slot, h, re, im):
        rows = part[h]
        tr = t_eff[li, slot, 0, rows, :].astype(F32)
        ti = t_eff[li, slot, 1, rows, :].astype(F32)
        right_forward(h, *conj_times(tr, ti, re, im))

    for li in (0, 1):
        g_own[li] = jnp.zeros((2, TILE, TILE), F32)
        for kind in range(3):
            g_alt[li, kind] = jnp.zeros((2, TILE, TILE), F32)

    def one_slot(slot, carry):
        @pl.when(slot == 0)
        def _():
            loads[5].wait()
            for c in t_copies(1):
                c.wait_recv()
            for s in (0, 1):
                window(1, s)

        for h in (0, 1):
            @pl.when(d < last)
            def _():
                w_copy(slot, h).wait_recv()

            through(1, slot, h, waves[slot, h, 0], waves[slot, h, 1])
        spectrum()
        for h in (0, 1):
            def keep(k, low, high, h=h):
                middle[slot, h, k, :, :HALF] = low
                middle[slot, h, k, :, HALF:] = high

            right_inverse(h, keep)

        @pl.when(slot == 0)
        def _():
            for c in t_copies(0):
                c.wait_recv()
            for s in (0, 1):
                window(0, s)

        @pl.when(d > 0)
        def _():
            for h in (0, 1):
                through(0, slot, h, middle[slot, h, 0], middle[slot, h, 1])
            spectrum()
            for h in (0, 1):
                def keep(k, low, high, h=h):
                    sent[slot, h, k, :, :HALF] = low
                    sent[slot, h, k, :, HALF:] = high

                right_inverse(h, keep)
                w_copy(slot, h).start()

        for li in (1, 0):
            wave = waves if li == 1 else middle
            for h in (0, 1):
                rows = part[h]
                own_x, own_y, alt_x, alt_y = masks(slot, h)
                er = inc[li, slot, 0, rows, :].astype(F32)
                ei = inc[li, slot, 1, rows, :].astype(F32)
                terms = conj_times(er, ei, wave[slot, h, 0], wave[slot, h, 1])
                for k, term in enumerate(terms):
                    g_own[li, k, rows, :] += jnp.where(own_x & own_y, term, zero)
                    g_alt[li, 0, k, rows, :] += jnp.where(alt_x & own_y, term, zero)
                    g_alt[li, 1, k, rows, :] += jnp.where(own_x & alt_y, term, zero)
                    g_alt[li, 2, k, rows, :] += jnp.where(alt_x & alt_y, term, zero)
        return carry

    lax.fori_loop(0, 2, one_slot, 0)

    for li in (1, 0):
        for c in g_copies(li):
            c.start()
    outs = []
    for li in (1, 0):
        for c in g_copies(li):
            c.wait_recv()
        for k in (0, 1):
            g_own[li, k] = (g_own[li, k] + g_in[li, 0, k]) + (g_in[li, 1, k] + g_in[li, 2, k])
        outs.append(pltpu.make_async_copy(g_own.at[li], out_hbm.at[li], out_sem.at[li]))
        outs[-1].start()

    for li in (1, 0):
        for c in t_copies(li):
            c.wait_send()
        for c in g_copies(li):
            c.wait_send()

    @pl.when(d > 0)
    def _():
        for slot in (0, 1):
            for h in (0, 1):
                w_copy(slot, h).wait_send()

    for c in outs:
        c.wait()


def shards(transmission, incident, exit_adjoint, propagator_phase, scan_anchor, live_count):
    sizes = tuple(lax.axis_size(a) for a in ("depth", "sx", "sy"))
    slab = transmission.shape[0]
    rows, lanes = twiddles()
    any_space = pl.BlockSpec(memory_space=pl.ANY)
    smem = pl.BlockSpec(memory_space=pltpu.SMEM)
    plane = (TILE, TILE)
    dma = pltpu.SemaphoreType.DMA
    return pl.pallas_call(
        functools.partial(kernel, sizes),
        out_shape=jax.ShapeDtypeStruct(transmission.shape, F32),
        in_specs=[any_space] * 6 + [pl.BlockSpec(memory_space=pltpu.VMEM), smem, smem],
        out_specs=any_space,
        scratch_shapes=[
            pltpu.VMEM((slab, 2) + plane, BF16),
            pltpu.VMEM((slab, 3, 2) + plane, BF16),
            pltpu.VMEM((slab, 2, 2) + plane, BF16),
            pltpu.VMEM((slab, 2, 2) + plane, BF16),
            pltpu.VMEM((2, 2) + plane, BF16),
            pltpu.VMEM(plane, F32),
            pltpu.VMEM((2, 2, HALF, TILE), F32),
            pltpu.VMEM((4,) + plane, BF16),
            pltpu.VMEM((2, HALF, HALF), F32),
            pltpu.VMEM((2, 2, 2, HALF, TILE), F32),
            pltpu.VMEM((2, 2, 2, HALF, TILE), F32),
            pltpu.VMEM((2, 2, 2, HALF, TILE), F32),
            pltpu.VMEM((2, 2, HALF, TILE), F32),
            pltpu.VMEM((2, 2, HALF, TILE), F32),
            pltpu.VMEM((slab, 2) + plane, F32),
            pltpu.VMEM((slab, 3, 2) + plane, F32),
            pltpu.VMEM((slab, 3, 2) + plane, F32),
            dma((6,)),
            dma((16,)),
            dma((16,)),
            dma((4,)),
            dma((4,)),
            dma((16,)),
            dma((16,)),
            dma((2,)),
        ],
        compiler_params=pltpu.CompilerParams(
            collective_id=0, has_side_effects=True, vmem_limit_bytes=60 * 1024 * 1024
        ),
    )(
        transmission,
        incident,
        exit_adjoint,
        propagator_phase,
        jnp.asarray(dft_tables()),
        jnp.asarray(rows),
        jnp.asarray(lanes),
        scan_anchor,
        live_count,
    )


def solution(mesh):
    placed = (
        P("depth", None, "sx", "sy"),
        P("depth", ("sx", "sy"), None, None, None),
        P(("sx", "sy"), None, None, None),
        P(),
        P(("sx", "sy"), None),
        P(("sx", "sy")),
    )
    return jax.shard_map(
        shards, mesh=mesh, in_specs=placed, out_specs=P("depth", None, "sx", "sy"), check_vma=False
    )
```

```python
import functools

import ml_dtypes
import numpy as np
import jax
import jax.numpy as jnp
from jax import lax
from jax.experimental import pallas as pl
from jax.experimental.pallas import tpu as pltpu
from jax.sharding import PartitionSpec as P

TILE = 256
HALF = 128
GROUPS = HALF // 8
CODED = HALF + 8
MESH = pl.DeviceIdType.MESH
F32 = jnp.float32
BF16 = jnp.bfloat16


def dft_tables():
    n = np.arange(HALF)
    angle = 2.0 * np.pi * ((n[:, None] * n[None, :]) % HALF) / HALF
    c, s = np.cos(angle) / 16.0, np.sin(angle) / 16.0
    m = np.block([[c, s], [-s, c]])
    out = []
    for a in (m, m.T):
        head = a.astype(ml_dtypes.bfloat16)
        out += [head, (a - head.astype(np.float64)).astype(ml_dtypes.bfloat16)]
    return np.stack(out)


def twiddles():
    n = 2.0 * np.pi * np.arange(HALF) / TILE
    rows = np.stack([np.cos(n), np.sin(n)])
    return (
        np.broadcast_to(rows[:, :, None], (2, HALF, HALF)).astype(np.float32),
        np.broadcast_to(rows[:, None, :], (2, 8, HALF)).astype(np.float32),
    )


def halves(x):
    head = x.astype(BF16)
    return head, (x - head.astype(F32)).astype(BF16)


def conj_times(ar, ai, br, bi):
    return ar * br + ai * bi, ar * bi - ai * br


def spread(x):
    return jnp.concatenate([x] * GROUPS, axis=0)


def coded(re, im):
    top = jnp.maximum(jnp.abs(re), jnp.abs(im))
    parts = [top[8 * g : 8 * g + 8] for g in range(GROUPS)]
    while len(parts) > 1:
        parts = [jnp.maximum(a, b) for a, b in zip(parts[::2], parts[1::2])]
    steps = (jnp.log2(jnp.maximum(parts[0], 1e-33)) * 8.0).astype(jnp.int32) + 2
    unit = spread(32767.0 / jnp.exp2(steps.astype(F32) * 0.125))
    high = (re * unit + 32768.5).astype(jnp.int32)
    low = (im * unit + 32768.5).astype(jnp.int32)
    return jnp.concatenate([(high << 16) | low, steps], axis=0)


def decoded(words):
    unit = spread(jnp.exp2(words[HALF:].astype(F32) * 0.125) * (1.0 / 32767.0))
    body = words[:HALF]
    high = ((body >> 16) & 65535).astype(F32) - 32768.0
    low = (body & 65535).astype(F32) - 32768.0
    return high * unit, low * unit


def dot(a, b):
    return jnp.dot(a, b, preferred_element_type=F32)


def kernel(
    sizes,
    t_hbm,
    inc_hbm,
    exit_hbm,
    phase_hbm,
    m_hbm,
    rows_hbm,
    lane_ref,
    anchor_ref,
    live_ref,
    out_hbm,
    t_own,
    t_alt,
    t_eff,
    inc,
    exit_v,
    phase,
    rot,
    m_v,
    rows_v,
    waves,
    middle,
    words_in,
    words_out,
    zbuf,
    ebuf,
    g_own,
    g_alt,
    g_out,
    g_in,
    load_sem,
    t_send,
    t_recv,
    w_send,
    w_recv,
    g_send,
    g_recv,
    out_sem,
    go,
):
    n_depth, n_sx, n_sy = sizes
    d, sx, sy = lax.axis_index("depth"), lax.axis_index("sx"), lax.axis_index("sy")
    last = n_depth - 1

    def at(dx, dy):
        return (d, lax.rem(sx + dx + n_sx, n_sx), lax.rem(sy + dy + n_sy, n_sy))

    around = [(i, j) for i in (-1, 0, 1) for j in (-1, 0, 1) if (i, j) != (0, 0)]

    loads = [
        pltpu.make_async_copy(src, dst, load_sem.at[i])
        for i, (src, dst) in enumerate(
            [
                (phase_hbm, phase),
                (m_hbm, m_v),
                (rows_hbm, rows_v),
                (exit_hbm, exit_v),
                (inc_hbm, inc),
                (t_hbm, t_own),
            ]
        )
    ]
    for c in loads:
        c.start()

    barrier = pltpu.get_barrier_semaphore()
    for i, j in around:
        pl.semaphore_signal(barrier, inc=1, device_id=at(i, j), device_id_type=MESH)

    for step in (1, last):
        near = (lax.rem(d + step, n_depth), sx, sy)
        pl.semaphore_signal(barrier, inc=1, device_id=near, device_id_type=MESH)
    pl.semaphore_wait(barrier, len(around) + 2)

    full = pl.ds(0, TILE)
    part = [pl.ds(0, HALF), pl.ds(HALF, HALF)]
    toward = [-1, 1]
    pieces = (
        [(0, part[p], full, (toward[p], 0)) for p in (0, 1)]
        + [(1, full, part[q], (0, toward[q])) for q in (0, 1)]
        + [(2, part[p], part[q], (toward[p], toward[q])) for p in (0, 1) for q in (0, 1)]
    )

    both = pl.ds(0, 2)
    one = [pl.ds(0, 1), pl.ds(1, 1)]
    blocks = (
        [(0, (one[p], both), (toward[p], 0)) for p in (0, 1)]
        + [(1, (both, one[q]), (0, toward[q])) for q in (0, 1)]
        + [(2, (one[p], one[q]), (toward[p], toward[q])) for p in (0, 1) for q in (0, 1)]
    )

    def t_copies(li):
        return [
            pltpu.make_async_remote_copy(
                src_ref=t_hbm.at[li, :, rows, lanes],
                dst_ref=t_alt.at[li, kind, :, rows, lanes],
                send_sem=t_send.at[li * 8 + i],
                recv_sem=t_recv.at[li * 8 + i],
                device_id=at(*way),
                device_id_type=MESH,
            )
            for i, (kind, rows, lanes, way) in enumerate(pieces)
        ]

    def g_copies(li):
        return [
            pltpu.make_async_remote_copy(
                src_ref=g_out.at[li, kind, block[0], block[1]],
                dst_ref=g_in.at[li, kind, block[0], block[1]],
                send_sem=g_send.at[li * 8 + i],
                recv_sem=g_recv.at[li * 8 + i],
                device_id=at(-way[0], -way[1]),
                device_id_type=MESH,
            )
            for i, (kind, block, way) in enumerate(blocks)
        ]

    def w_copy(slot, h):
        return pltpu.make_async_remote_copy(
            src_ref=words_out.at[slot, h],
            dst_ref=words_in.at[slot, h],
            send_sem=w_send.at[slot * 2 + h],
            recv_sem=w_recv.at[slot * 2 + h],
            device_id=(lax.rem(d + last, n_depth), sx, sy),
            device_id_type=MESH,
        )

    odd = lax.rem(d, 2) == 1

    def share():
        for li in (1, 0):
            for c in t_copies(li):
                c.start()

    @pl.when(odd)
    def _():
        share()

    def offsets(slot):
        return anchor_ref[slot, 0] - sx * TILE, anchor_ref[slot, 1] - sy * TILE

    def spans(slot):
        ax, ay = offsets(slot)
        out = []
        for a, k, n in ((ax, sx, n_sx), (ay, sy, n_sy)):
            low, high = jnp.maximum(a, 0), TILE + jnp.minimum(a, 0)
            out.append((low, high, jnp.where(k < n - 1, low, 0), jnp.where(k > 0, high, TILE)))
        return out

    def masks(slot, h):
        (lx, hx, olx, ohx), (ly, hy, oly, ohy) = spans(slot)
        r = lax.broadcasted_iota(jnp.int32, (HALF, TILE), 0) + h * HALF
        c = lax.broadcasted_iota(jnp.int32, (HALF, TILE), 1)
        own_x = (r >= lx) & (r < hx)
        own_y = (c >= ly) & (c < hy)
        alt_x = (r < olx) | (r >= ohx)
        alt_y = (c < oly) | (c >= ohy)
        return own_x, own_y, alt_x, alt_y

    def rolled(slot, fields):
        ax, ay = offsets(slot)
        i = lax.broadcasted_iota(jnp.int32, (TILE, TILE), 0)
        j = lax.broadcasted_iota(jnp.int32, (TILE, TILE), 1)
        by_rows = jnp.where(((j + ax - i) & (TILE - 1)) == 0, 1.0, 0.0).astype(BF16)
        by_lanes = jnp.where(((i + ay - j) & (TILE - 1)) == 0, 1.0, 0.0).astype(BF16)
        return [dot(by_rows, dot(f, by_lanes).astype(BF16)) for f in fields]

    for c in loads[:5]:
        c.wait()

    @pl.when(d == last)
    def _():
        for slot in (0, 1):
            alive = jnp.where(slot < live_ref[0], 1.0, 0.0).astype(F32)
            for k, f in enumerate(rolled(slot, [exit_v[slot, 0], exit_v[slot, 1]])):
                for h in (0, 1):
                    waves[slot, h, k] = f[h * HALF : (h + 1) * HALF] * alive

    i = lax.broadcasted_iota(jnp.int32, (TILE, TILE), 0)
    j = lax.broadcasted_iota(jnp.int32, (TILE, TILE), 1)
    deal = jnp.where(i == jnp.where(j < HALF, 2 * j, 2 * j - (TILE - 1)), 1.0, 0.0).astype(BF16)
    deal_rows = jnp.where(j == jnp.where(i < HALF, 2 * i, 2 * i - (TILE - 1)), 1.0, 0.0).astype(BF16)
    p = phase[...]
    p0 = p.astype(BF16)
    p1, p2 = halves(p - p0.astype(F32))
    f0, f1, f2 = [dot(deal_rows, dot(q, deal).astype(BF16)) for q in (p0, p1, p2)]
    phase[...] = (f0 + f1) + f2
    for h in (0, 1):
        ordered = phase[part[h], :]
        rot[0, h] = jnp.cos(ordered)
        rot[1, h] = jnp.sin(ordered)

    def roll_incident(slot):
        got = rolled(slot, [inc[li, slot, k] for li in (0, 1) for k in (0, 1)])
        for n, f in enumerate(got):
            inc[n // 2, slot, n % 2] = f.astype(BF16)

    for slot in (0, 1):
        roll_incident(slot)

    zero = jnp.zeros((HALF, TILE), F32)

    def window(li, slot):
        for h in (0, 1):
            own_x, own_y, alt_x, alt_y = masks(slot, h)
            rows = part[h]
            for k in (0, 1):
                here = t_own[li, k, rows, :].astype(F32)
                tx = t_alt[li, 0, k, rows, :].astype(F32)
                ty = t_alt[li, 1, k, rows, :].astype(F32)
                txy = t_alt[li, 2, k, rows, :].astype(F32)
                inner = jnp.where(own_y, here, jnp.where(alt_y, ty, zero))
                outer = jnp.where(own_y, tx, jnp.where(alt_y, txy, zero))
                t_eff[li, slot, k, rows, :] = jnp.where(
                    own_x, inner, jnp.where(alt_x, outer, zero)
                ).astype(BF16)

    cl, sl = lane_ref[0, 0:1, :], lane_ref[1, 0:1, :]

    def right(z, first):
        head, tail = halves(z)
        table = jnp.concatenate([m_v[first], m_v[first], m_v[first + 1]], axis=0)
        return dot(jnp.concatenate([head, tail, head], axis=1), table)

    def left(z, first):
        head, tail = halves(z)
        table = jnp.concatenate([m_v[first], m_v[first + 1], m_v[first]], axis=1)
        return dot(table, jnp.concatenate([head, head, tail], axis=0))

    def right_forward(h, re, im):
        sr, dr = re[:, :HALF] + re[:, HALF:], re[:, :HALF] - re[:, HALF:]
        si, di = im[:, :HALF] + im[:, HALF:], im[:, :HALF] - im[:, HALF:]
        tr, ti = dr * cl + di * sl, di * cl - dr * sl
        z = jnp.concatenate(
            [jnp.concatenate([sr, si], axis=1), jnp.concatenate([tr, ti], axis=1)], axis=0
        )
        y = right(z, 2)
        zbuf[h, 0, :, :HALF] = y[:HALF, :HALF]
        zbuf[h, 0, :, HALF:] = y[HALF:, :HALF]
        zbuf[h, 1, :, :HALF] = y[:HALF, HALF:]
        zbuf[h, 1, :, HALF:] = y[HALF:, HALF:]

    def row_twiddle():
        c, s = rows_v[0], rows_v[1]
        return jnp.concatenate([c, c], axis=1), jnp.concatenate([s, s], axis=1)

    def spectrum():
        for h in (0, 1):
            if h == 0:
                zr, zi = zbuf[0, 0] + zbuf[1, 0], zbuf[0, 1] + zbuf[1, 1]
            else:
                c, s = row_twiddle()
                dr, di = zbuf[0, 0] - zbuf[1, 0], zbuf[0, 1] - zbuf[1, 1]
                zr, zi = dr * c + di * s, di * c - dr * s
            x = left(jnp.concatenate([zr, zi], axis=0), 0)
            xr, xi = x[:HALF], x[HALF:]
            cp, sp = rot[0, h], rot[1, h]
            y = jnp.concatenate([xr * cp + xi * sp, xi * cp - xr * sp], axis=0)
            e = left(y, 2)
            er, ei = e[:HALF], e[HALF:]
            if h == 1:
                er, ei = er * c - ei * s, ei * c + er * s
            ebuf[h, 0] = er
            ebuf[h, 1] = ei

    def right_inverse(h, store):
        if h == 0:
            vr, vi = ebuf[0, 0] + ebuf[1, 0], ebuf[0, 1] + ebuf[1, 1]
        else:
            vr, vi = ebuf[0, 0] - ebuf[1, 0], ebuf[0, 1] - ebuf[1, 1]
        z = jnp.concatenate(
            [
                jnp.concatenate([vr[:, :HALF], vi[:, :HALF]], axis=1),
                jnp.concatenate([vr[:, HALF:], vi[:, HALF:]], axis=1),
            ],
            axis=0,
        )
        y = right(z, 0)
        er, ei, orr, oi = y[:HALF, :HALF], y[:HALF, HALF:], y[HALF:, :HALF], y[HALF:, HALF:]
        tr, ti = orr * cl - oi * sl, oi * cl + orr * sl
        store(er + tr, er - tr, ei + ti, ei - ti)

    def through(li, slot, h, re, im):
        rows = part[h]
        tr = t_eff[li, slot, 0, rows, :].astype(F32)
        ti = t_eff[li, slot, 1, rows, :].astype(F32)
        right_forward(h, *conj_times(tr, ti, re, im))

    for li in (0, 1):
        g_own[li] = jnp.zeros((2, TILE, TILE), F32)
        for kind in range(3):
            g_alt[li, kind] = jnp.zeros((2, TILE, TILE), F32)

    def gradient(li, slot):
        wave = waves if li == 1 else middle
        for h in (0, 1):
            rows = part[h]
            own_x, own_y, alt_x, alt_y = masks(slot, h)
            er = inc[li, slot, 0, rows, :].astype(F32)
            ei = inc[li, slot, 1, rows, :].astype(F32)
            terms = conj_times(er, ei, wave[slot, h, 0], wave[slot, h, 1])
            for k, term in enumerate(terms):
                g_own[li, k, rows, :] += jnp.where(own_x & own_y, term, zero)
                g_alt[li, 0, k, rows, :] += jnp.where(alt_x & own_y, term, zero)
                g_alt[li, 1, k, rows, :] += jnp.where(own_x & alt_y, term, zero)
                g_alt[li, 2, k, rows, :] += jnp.where(alt_x & alt_y, term, zero)

    def hand_over(li):
        for kind in (2, 0, 1):
            for p in (0, 1):
                for q in (0, 1):
                    g_out[li, kind, p, q] = coded(
                        g_alt[li, kind, 0, part[p], part[q]], g_alt[li, kind, 1, part[p], part[q]]
                    )
        for c in g_copies(li):
            c.start()

    def apply_layer(li, slot, source, store, done):
        for h in (0, 1):
            through(li, slot, h, source[slot, h, 0], source[slot, h, 1])
        spectrum()
        for h in (0, 1):
            right_inverse(h, functools.partial(store, h))
            done(h)

    loads[5].wait()

    @pl.when(odd)
    def _():
        for c in t_copies(1):
            c.wait_recv()
        pl.semaphore_signal(go, inc=1, device_id=(d - 1, sx, sy), device_id_type=MESH)

    @pl.when(jnp.logical_not(odd))
    def _():
        pl.semaphore_wait(go, 1)
        share()
        for c in t_copies(1):
            c.wait_recv()

    for slot in (0, 1):
        window(1, slot)

    early = d < 2

    def one_slot(slot, carry):
        @pl.when(d < last)
        def _():
            for h in (0, 1):
                w_copy(slot, h).wait_recv()
                for q in (0, 1):
                    re, im = decoded(words_in[slot, h, q])
                    waves[slot, h, 0, :, part[q]] = re
                    waves[slot, h, 1, :, part[q]] = im

        @pl.when(early)
        def _():
            gradient(1, slot)

            @pl.when(slot == 1)
            def _():
                hand_over(1)

        def keep(h, lr, hr, li_, hi_):
            middle[slot, h, 0, :, :HALF] = lr
            middle[slot, h, 0, :, HALF:] = hr
            middle[slot, h, 1, :, :HALF] = li_
            middle[slot, h, 1, :, HALF:] = hi_

        apply_layer(1, slot, waves, keep, lambda h: None)

        @pl.when(slot == 0)
        def _():
            for c in t_copies(0):
                c.wait_recv()
            for s in (0, 1):
                window(0, s)

        @pl.when(early)
        def _():
            gradient(0, slot)

            @pl.when(slot == 1)
            def _():
                hand_over(0)

        @pl.when(d > 0)
        def _():
            def encode(h, lr, hr, li_, hi_):
                words_out[slot, h, 0] = coded(lr, li_)
                words_out[slot, h, 1] = coded(hr, hi_)

            apply_layer(0, slot, middle, encode, lambda h: w_copy(slot, h).start())

        return carry

    lax.fori_loop(0, 2, one_slot, 0)

    @pl.when(jnp.logical_not(early))
    def _():
        for li in (1, 0):
            def both_slots(slot, carry, li=li):
                gradient(li, slot)
                return carry

            lax.fori_loop(0, 2, both_slots, 0)
            hand_over(li)

    outs = []
    for li in (1, 0):
        for c in g_copies(li):
            c.wait_recv()
        for p in (0, 1):
            for q in (0, 1):
                got = [decoded(g_in[li, kind, p, q]) for kind in range(3)]
                for k in (0, 1):
                    total = (got[0][k] + got[1][k]) + got[2][k]
                    g_own[li, k, part[p], part[q]] += total
        outs.append(pltpu.make_async_copy(g_own.at[li], out_hbm.at[li], out_sem.at[li]))
        outs[-1].start()

    for li in (1, 0):
        for c in t_copies(li):
            c.wait_send()
        for c in g_copies(li):
            c.wait_send()

    @pl.when(d > 0)
    def _():
        for slot in (0, 1):
            for h in (0, 1):
                w_copy(slot, h).wait_send()

    for c in outs:
        c.wait()


def shards(transmission, incident, exit_adjoint, propagator_phase, scan_anchor, live_count):
    sizes = tuple(lax.axis_size(a) for a in ("depth", "sx", "sy"))
    slab = transmission.shape[0]
    rows, lanes = twiddles()
    any_space = pl.BlockSpec(memory_space=pl.ANY)
    smem = pl.BlockSpec(memory_space=pltpu.SMEM)
    plane = (TILE, TILE)
    dma = pltpu.SemaphoreType.DMA
    return pl.pallas_call(
        functools.partial(kernel, sizes),
        out_shape=jax.ShapeDtypeStruct(transmission.shape, F32),
        in_specs=[any_space] * 6 + [pl.BlockSpec(memory_space=pltpu.VMEM), smem, smem],
        out_specs=any_space,
        scratch_shapes=[
            pltpu.VMEM((slab, 2) + plane, BF16),
            pltpu.VMEM((slab, 3, 2) + plane, BF16),
            pltpu.VMEM((slab, 2, 2) + plane, BF16),
            pltpu.VMEM((slab, 2, 2) + plane, BF16),
            pltpu.VMEM((2, 2) + plane, BF16),
            pltpu.VMEM(plane, F32),
            pltpu.VMEM((2, 2, HALF, TILE), F32),
            pltpu.VMEM((4,) + plane, BF16),
            pltpu.VMEM((2, HALF, HALF), F32),
            pltpu.VMEM((2, 2, 2, HALF, TILE), F32),
            pltpu.VMEM((2, 2, 2, HALF, TILE), F32),
            pltpu.VMEM((2, 2, 2, CODED, HALF), jnp.int32),
            pltpu.VMEM((2, 2, 2, CODED, HALF), jnp.int32),
            pltpu.VMEM((2, 2, HALF, TILE), F32),
            pltpu.VMEM((2, 2, HALF, TILE), F32),
            pltpu.VMEM((slab, 2) + plane, F32),
            pltpu.VMEM((slab, 3, 2) + plane, F32),
            pltpu.VMEM((slab, 3, 2, 2, CODED, HALF), jnp.int32),
            pltpu.VMEM((slab, 3, 2, 2, CODED, HALF), jnp.int32),
            dma((6,)),
            dma((16,)),
            dma((16,)),
            dma((4,)),
            dma((4,)),
            dma((16,)),
            dma((16,)),
            dma((2,)),
            pltpu.SemaphoreType.REGULAR,
        ],
        compiler_params=pltpu.CompilerParams(
            collective_id=0, has_side_effects=True, vmem_limit_bytes=60 * 1024 * 1024
        ),
    )(
        transmission,
        incident,
        exit_adjoint,
        propagator_phase,
        jnp.asarray(dft_tables()),
        jnp.asarray(rows),
        jnp.asarray(lanes),
        scan_anchor,
        live_count,
    )


def solution(mesh):
    placed = (
        P("depth", None, "sx", "sy"),
        P("depth", ("sx", "sy"), None, None, None),
        P(("sx", "sy"), None, None, None),
        P(),
        P(("sx", "sy"), None),
        P(("sx", "sy")),
    )
    return jax.shard_map(
        shards, mesh=mesh, in_specs=placed, out_specs=P("depth", None, "sx", "sy"), check_vma=False
    )
```

```python
import functools

import ml_dtypes
import numpy as np
import jax
import jax.numpy as jnp
from jax import lax
from jax.experimental import pallas as pl
from jax.experimental.pallas import tpu as pltpu
from jax.sharding import PartitionSpec as P

TILE = 256
HALF = 128
GROUPS = HALF // 8
CODED = HALF + 8
MESH = pl.DeviceIdType.MESH
F32 = jnp.float32
BF16 = jnp.bfloat16


def dft_tables():
    n = np.arange(HALF)
    out = []
    for odd in (0, 1):
        angle = 2.0 * np.pi * (((2 * n[:, None] + odd) * n[None, :]) % TILE) / TILE
        c, s = np.cos(angle) / 16.0, np.sin(angle) / 16.0
        m = np.block([[c, s], [-s, c]])
        for a in (m, m.T):
            head = a.astype(ml_dtypes.bfloat16)
            out += [head, (a - head.astype(np.float64)).astype(ml_dtypes.bfloat16)]
    return np.stack(out)


def halves(x):
    head = x.astype(BF16)
    return head, (x - head.astype(F32)).astype(BF16)


def conj_times(ar, ai, br, bi):
    return ar * br + ai * bi, ar * bi - ai * br


def spread(x):
    return jnp.concatenate([x] * GROUPS, axis=0)


def coded(re, im):
    top = jnp.maximum(jnp.abs(re), jnp.abs(im))
    parts = [top[8 * g : 8 * g + 8] for g in range(GROUPS)]
    while len(parts) > 1:
        parts = [jnp.maximum(a, b) for a, b in zip(parts[::2], parts[1::2])]
    steps = (jnp.log2(jnp.maximum(parts[0], 1e-33)) * 8.0).astype(jnp.int32) + 2
    unit = spread(32767.0 / jnp.exp2(steps.astype(F32) * 0.125))
    high = (re * unit + 32768.5).astype(jnp.int32)
    low = (im * unit + 32768.5).astype(jnp.int32)
    return jnp.concatenate([(high << 16) | low, steps], axis=0)


def decoded(words, weight=1.0 / 32767.0):
    unit = spread(jnp.exp2(words[HALF:].astype(F32) * 0.125) * weight)
    body = words[:HALF]
    high = ((body >> 16) & 65535).astype(F32) - 32768.0
    low = (body & 65535).astype(F32) - 32768.0
    return high * unit, low * unit


def dot(a, b):
    return jnp.dot(a, b, preferred_element_type=F32)


def kernel(
    sizes,
    t_hbm,
    inc_hbm,
    exit_hbm,
    phase_hbm,
    m_hbm,
    anchor_ref,
    live_ref,
    own,
    t_own,
    t_alt,
    t_eff,
    inc,
    exit_v,
    phase,
    rot,
    m_v,
    waves,
    middle,
    words_in,
    words_out,
    g_alt,
    g_out,
    g_in,
    load_sem,
    t_send,
    t_recv,
    w_send,
    w_recv,
    g_send,
    g_recv,
    go,
):
    n_depth, n_sx, n_sy = sizes
    d, sx, sy = lax.axis_index("depth"), lax.axis_index("sx"), lax.axis_index("sy")
    last = n_depth - 1

    def at(dx, dy):
        return (d, lax.rem(sx + dx + n_sx, n_sx), lax.rem(sy + dy + n_sy, n_sy))

    around = [(i, j) for i in (-1, 0, 1) for j in (-1, 0, 1) if (i, j) != (0, 0)]

    loads = [
        pltpu.make_async_copy(src, dst, load_sem.at[i])
        for i, (src, dst) in enumerate(
            [
                (phase_hbm, phase),
                (m_hbm, m_v),
                (exit_hbm, exit_v),
                (inc_hbm, inc),
                (t_hbm, t_own),
            ]
        )
    ]
    for c in loads:
        c.start()

    barrier = pltpu.get_barrier_semaphore()
    for i, j in around:
        pl.semaphore_signal(barrier, inc=1, device_id=at(i, j), device_id_type=MESH)

    for step in (1, last):
        near = (lax.rem(d + step, n_depth), sx, sy)
        pl.semaphore_signal(barrier, inc=1, device_id=near, device_id_type=MESH)
    pl.semaphore_wait(barrier, len(around) + 2)

    full = pl.ds(0, TILE)
    part = [pl.ds(0, HALF), pl.ds(HALF, HALF)]
    toward = [-1, 1]
    pieces = (
        [(0, part[p], full, (toward[p], 0)) for p in (0, 1)]
        + [(1, full, part[q], (0, toward[q])) for q in (0, 1)]
        + [(2, part[p], part[q], (toward[p], toward[q])) for p in (0, 1) for q in (0, 1)]
    )

    both = pl.ds(0, 2)
    one = [pl.ds(0, 1), pl.ds(1, 1)]
    blocks = (
        [(0, (one[p], both), (toward[p], 0)) for p in (0, 1)]
        + [(1, (both, one[q]), (0, toward[q])) for q in (0, 1)]
        + [(2, (one[p], one[q]), (toward[p], toward[q])) for p in (0, 1) for q in (0, 1)]
    )

    def t_copies(li):
        return [
            pltpu.make_async_remote_copy(
                src_ref=t_hbm.at[li, :, rows, lanes],
                dst_ref=t_alt.at[li, kind, :, rows, lanes],
                send_sem=t_send.at[li * 8 + i],
                recv_sem=t_recv.at[li * 8 + i],
                device_id=at(*way),
                device_id_type=MESH,
            )
            for i, (kind, rows, lanes, way) in enumerate(pieces)
        ]

    def g_copies(li):
        return [
            pltpu.make_async_remote_copy(
                src_ref=g_out.at[li, kind, block[0], block[1]],
                dst_ref=g_in.at[li, kind, block[0], block[1]],
                send_sem=g_send.at[li * 8 + i],
                recv_sem=g_recv.at[li * 8 + i],
                device_id=at(-way[0], -way[1]),
                device_id_type=MESH,
            )
            for i, (kind, block, way) in enumerate(blocks)
        ]

    def w_copy(slot, h):
        return pltpu.make_async_remote_copy(
            src_ref=words_out.at[slot, h],
            dst_ref=words_in.at[slot, h],
            send_sem=w_send.at[slot * 2 + h],
            recv_sem=w_recv.at[slot * 2 + h],
            device_id=(lax.rem(d + last, n_depth), sx, sy),
            device_id_type=MESH,
        )

    odd = lax.rem(d, 2) == 1

    def share():
        for li in (1, 0):
            for c in t_copies(li):
                c.start()

    @pl.when(odd)
    def _():
        share()

    def offsets(slot):
        return anchor_ref[slot, 0] - sx * TILE, anchor_ref[slot, 1] - sy * TILE

    quads = [(0, 0), (0, 1), (1, 0), (1, 1)]

    def masks(slot, p, q):
        out = []
        for a, half, dim in zip(offsets(slot), (p, q), (0, 1)):
            k = lax.broadcasted_iota(jnp.int32, (HALF, HALF), dim)
            out.append(k >= a if half == 0 else k < a + HALF)
        return out

    def rolled(slot, fields):
        ax, ay = offsets(slot)
        i = lax.broadcasted_iota(jnp.int32, (TILE, TILE), 0)
        j = lax.broadcasted_iota(jnp.int32, (TILE, TILE), 1)
        by_rows = jnp.where(((j + ax - i) & (TILE - 1)) == 0, 1.0, 0.0).astype(BF16)
        by_lanes = jnp.where(((i + ay - j) & (TILE - 1)) == 0, 1.0, 0.0).astype(BF16)
        return [dot(by_rows, dot(f, by_lanes).astype(BF16)) for f in fields]

    for c in loads[:4]:
        c.wait()

    @pl.when(d == last)
    def _():
        for slot in (0, 1):
            alive = jnp.where(slot < live_ref[0, 0], 1.0, 0.0).astype(F32)
            for k, f in enumerate(rolled(slot, [exit_v[slot, 0], exit_v[slot, 1]])):
                for h in (0, 1):
                    waves[slot, h, k] = f[h * HALF : (h + 1) * HALF] * alive

    i = lax.broadcasted_iota(jnp.int32, (TILE, TILE), 0)
    j = lax.broadcasted_iota(jnp.int32, (TILE, TILE), 1)
    deal = jnp.where(i == jnp.where(j < HALF, 2 * j, 2 * j - (TILE - 1)), 1.0, 0.0).astype(BF16)
    deal_rows = jnp.where(j == jnp.where(i < HALF, 2 * i, 2 * i - (TILE - 1)), 1.0, 0.0).astype(BF16)
    p = phase[...]
    p0 = p.astype(BF16)
    p1, p2 = halves(p - p0.astype(F32))
    f0, f1, f2 = [dot(deal_rows, dot(q, deal).astype(BF16)) for q in (p0, p1, p2)]
    phase[...] = (f0 + f1) + f2
    for h in (0, 1):
        ordered = phase[part[h], :]
        rot[0, h] = jnp.cos(ordered)
        rot[1, h] = jnp.sin(ordered)

    def roll_incident(slot):
        got = rolled(slot, [inc[li, slot, k] for li in (0, 1) for k in (0, 1)])
        for n, f in enumerate(got):
            inc[n // 2, slot, n % 2] = f.astype(BF16)

    for slot in (0, 1):
        roll_incident(slot)

    zero = jnp.zeros((HALF, HALF), F32)

    def window(li, slot):
        for p, q in quads:
            on_x, on_y = masks(slot, p, q)
            spot = (part[p], part[q])
            for k in (0, 1):
                here = t_own[(li, k) + spot].astype(F32)
                tx, ty, txy = [t_alt[(li, kind, k) + spot].astype(F32) for kind in range(3)]
                t_eff[(li, slot, k) + spot] = jnp.where(
                    on_x, jnp.where(on_y, here, ty), jnp.where(on_y, tx, txy)
                ).astype(BF16)

    def border(li):
        for p in (0, 1):
            edge_x, edge_y = [(n - 1, 0)[p] for n in (n_sx, n_sy)]

            @pl.when(sx == edge_x)
            def _(p=p):
                for kind in (0, 2):
                    t_alt[li, kind, :, part[p], :] = jnp.zeros((2, HALF, TILE), BF16)

            @pl.when(sy == edge_y)
            def _(p=p):
                for kind in (1, 2):
                    t_alt[li, kind, :, :, part[p]] = jnp.zeros((2, TILE, HALF), BF16)

    def windows(li):
        for c in t_copies(li)[1 if li == 1 else 0 :]:
            c.wait_recv()
        border(li)
        for slot in (0, 1):
            window(li, slot)

    def beside(a, b):
        return jnp.concatenate([a, b], axis=1)

    def above(a, b):
        return jnp.concatenate([a, b], axis=0)

    def right(z, first):
        head, tail = halves(z)
        table = jnp.concatenate([m_v[first], m_v[first], m_v[first + 1]], axis=0)
        return dot(jnp.concatenate([head, tail, head], axis=1), table)

    def left(z, first):
        head, tail = halves(z)
        table = jnp.concatenate([m_v[first], m_v[first + 1], m_v[first]], axis=1)
        return dot(table, jnp.concatenate([head, head, tail], axis=0))

    def propagated(fields):
        a = [beside(re[:, :HALF], im[:, :HALF]) for re, im in fields]
        b = [beside(re[:, HALF:], im[:, HALF:]) for re, im in fields]
        deal = [above(a[0] + b[0], a[1] + b[1]), above(a[0] - b[0], a[1] - b[1])]
        ys = [right(deal[g], 4 * g + 2) for g in (0, 1)]
        res = beside(ys[0][:, :HALF], ys[1][:, :HALF])
        ims = beside(ys[0][:, HALF:], ys[1][:, HALF:])
        upper, lower = above(res[:HALF], ims[:HALF]), above(res[HALF:], ims[HALF:])
        xs = [left(z, 4 * h) for h, z in enumerate((upper + lower, upper - lower))]
        turned = []
        for h, x in enumerate(xs):
            xr, xi = x[:HALF], x[HALF:]
            cp, sp = rot[0, h], rot[1, h]
            turned.append(above(xr * cp + xi * sp, xi * cp - xr * sp))
        es = [left(z, 4 * h + 2) for h, z in enumerate(turned)]
        upper, lower = es[0] + es[1], es[0] - es[1]
        out = []
        for g in (0, 1):
            lanes = slice(g * HALF, (g + 1) * HALF)
            z = above(
                beside(upper[:HALF, lanes], upper[HALF:, lanes]),
                beside(lower[:HALF, lanes], lower[HALF:, lanes]),
            )
            out.append(right(z, 4 * g))
        return out

    def finish(joined, store):
        for h in (0, 1):
            e, o = [j[h * HALF : (h + 1) * HALF] for j in joined]
            low, high = e + o, e - o
            store(h, low[:, :HALF], high[:, :HALF], low[:, HALF:], high[:, HALF:])

    def through(li, slot, h, re, im):
        rows = part[h]
        tr = t_eff[li, slot, 0, rows, :].astype(F32)
        ti = t_eff[li, slot, 1, rows, :].astype(F32)
        return conj_times(tr, ti, re, im)

    def shares(li, slot, p, q):
        wave = waves if li == 1 else middle
        er = inc[li, slot, 0, part[p], part[q]].astype(F32)
        ei = inc[li, slot, 1, part[p], part[q]].astype(F32)
        on_x, on_y = masks(slot, p, q)
        out = []
        for t in conj_times(er, ei, wave[slot, p, 0, :, part[q]], wave[slot, p, 1, :, part[q]]):
            inside = jnp.where(on_x, t, zero)
            beyond = jnp.where(on_x, zero, t)
            out.append(
                [
                    jnp.where(on_y, inside, zero),
                    jnp.where(on_y, beyond, zero),
                    jnp.where(on_y, zero, inside),
                    jnp.where(on_y, zero, beyond),
                ]
            )
        return out

    def first_gradient(li):
        for p, q in quads:
            spot = (part[p], part[q])
            for k, t in enumerate(shares(li, 0, p, q)):
                own[(li, k) + spot] = t[0]
                for kind in range(3):
                    g_alt[(li, kind, k) + spot] = t[kind + 1]

    def second_gradient(li):
        copies = g_copies(li)
        for p, q in quads:
            spot = (part[p], part[q])
            re, im = shares(li, 1, p, q)
            for kind in (2, 0, 1):
                g_out[li, kind, p, q] = coded(
                    g_alt[(li, kind, 0) + spot] + re[kind + 1], g_alt[(li, kind, 1) + spot] + im[kind + 1]
                )
            copies[4 + 2 * p + q].start()
            if q == 1:
                copies[p].start()
            if p == 1:
                copies[2 + q].start()
            own[(li, 0) + spot] += re[0]
            own[(li, 1) + spot] += im[0]

    def gradient(li, slot):
        @pl.when(slot == 0)
        def _():
            first_gradient(li)

        @pl.when(slot == 1)
        def _():
            second_gradient(li)

    def apply_layer(li, slot, source, store):
        fields = [through(li, slot, h, source[slot, h, 0], source[slot, h, 1]) for h in (0, 1)]
        finish(propagated(fields), store)

    loads[4].wait()

    @pl.when(odd)
    def _():
        t_copies(1)[0].wait_recv()
        pl.semaphore_signal(go, inc=1, device_id=(d - 1, sx, sy), device_id_type=MESH)

    @pl.when(jnp.logical_not(odd))
    def _():
        pl.semaphore_wait(go, 1)
        share()
        t_copies(1)[0].wait_recv()

    windows(1)

    early = d < 2

    def one_slot(slot, carry):
        @pl.when(d < last)
        def _():
            for h in (0, 1):
                w_copy(slot, h).wait_recv()
                for q in (0, 1):
                    re, im = decoded(words_in[slot, h, q])
                    waves[slot, h, 0, :, part[q]] = re
                    waves[slot, h, 1, :, part[q]] = im

        @pl.when(early)
        def _():
            gradient(1, slot)

        def keep(h, lr, hr, li_, hi_):
            middle[slot, h, 0, :, :HALF] = lr
            middle[slot, h, 0, :, HALF:] = hr
            middle[slot, h, 1, :, :HALF] = li_
            middle[slot, h, 1, :, HALF:] = hi_

        apply_layer(1, slot, waves, keep)

        @pl.when(slot == 0)
        def _():
            windows(0)

        @pl.when(early)
        def _():
            gradient(0, slot)

        @pl.when(d > 0)
        def _():
            def encode(h, lr, hr, li_, hi_):
                words_out[slot, h, 0] = coded(lr, li_)
                words_out[slot, h, 1] = coded(hr, hi_)
                w_copy(slot, h).start()

            apply_layer(0, slot, middle, encode)

        return carry

    lax.fori_loop(0, 2, one_slot, 0)

    @pl.when(jnp.logical_not(early))
    def _():
        for li in (1, 0):
            first_gradient(li)
            second_gradient(li)

    for li in (1, 0):
        for c in t_copies(li):
            c.wait_send()

    @pl.when(d > 0)
    def _():
        for slot in (0, 1):
            for h in (0, 1):
                w_copy(slot, h).wait_send()

    from_x = [jnp.where(sx > 0, 1.0, 0.0), jnp.where(sx < n_sx - 1, 1.0, 0.0)]
    from_y = [jnp.where(sy > 0, 1.0, 0.0), jnp.where(sy < n_sy - 1, 1.0, 0.0)]
    for li in (1, 0):
        copies = g_copies(li)
        for p, q in quads:
            if q == 0:
                copies[p].wait_recv()
            if p == 0:
                copies[2 + q].wait_recv()
            copies[4 + 2 * p + q].wait_recv()
            weights = (from_x[p], from_y[q], from_x[p] * from_y[q])
            got = [decoded(g_in[li, kind, p, q], weights[kind] / 32767.0) for kind in range(3)]
            for k in (0, 1):
                own[li, k, part[p], part[q]] += (got[0][k] + got[1][k]) + got[2][k]

    for li in (1, 0):
        for c in g_copies(li):
            c.wait_send()


def shards(transmission, incident, exit_adjoint, propagator_phase, scan_anchor, live_count):
    sizes = tuple(lax.axis_size(a) for a in ("depth", "sx", "sy"))
    slab = transmission.shape[0]
    any_space = pl.BlockSpec(memory_space=pl.ANY)
    smem = pl.BlockSpec(memory_space=pltpu.SMEM)
    plane = (TILE, TILE)
    dma = pltpu.SemaphoreType.DMA
    return pl.pallas_call(
        functools.partial(kernel, sizes),
        out_shape=pltpu.VMEM(transmission.shape, F32),
        in_specs=[any_space] * 5 + [smem, smem],
        out_specs=pl.BlockSpec(memory_space=pltpu.VMEM),
        scratch_shapes=[
            pltpu.VMEM((slab, 2) + plane, BF16),
            pltpu.VMEM((slab, 3, 2) + plane, BF16),
            pltpu.VMEM((slab, 2, 2) + plane, BF16),
            pltpu.VMEM((slab, 2, 2) + plane, BF16),
            pltpu.VMEM((2, 2) + plane, BF16),
            pltpu.VMEM(plane, F32),
            pltpu.VMEM((2, 2, HALF, TILE), F32),
            pltpu.VMEM((8,) + plane, BF16),
            pltpu.VMEM((2, 2, 2, HALF, TILE), F32),
            pltpu.VMEM((2, 2, 2, HALF, TILE), F32),
            pltpu.VMEM((2, 2, 2, CODED, HALF), jnp.int32),
            pltpu.VMEM((2, 2, 2, CODED, HALF), jnp.int32),
            pltpu.VMEM((slab, 3, 2) + plane, F32),
            pltpu.VMEM((slab, 3, 2, 2, CODED, HALF), jnp.int32),
            pltpu.VMEM((slab, 3, 2, 2, CODED, HALF), jnp.int32),
            dma((5,)),
            dma((16,)),
            dma((16,)),
            dma((4,)),
            dma((4,)),
            dma((16,)),
            dma((16,)),
            pltpu.SemaphoreType.REGULAR,
        ],
        compiler_params=pltpu.CompilerParams(
            collective_id=0, has_side_effects=True, vmem_limit_bytes=60 * 1024 * 1024
        ),
    )(
        transmission,
        incident,
        exit_adjoint,
        propagator_phase,
        jnp.asarray(dft_tables()),
        scan_anchor,
        live_count[None],
    )


def solution(mesh):
    placed = (
        P("depth", None, "sx", "sy"),
        P("depth", ("sx", "sy"), None, None, None),
        P(("sx", "sy"), None, None, None),
        P(),
        P(("sx", "sy"), None),
        P(("sx", "sy")),
    )
    return jax.shard_map(
        shards, mesh=mesh, in_specs=placed, out_specs=P("depth", None, "sx", "sy"), check_vma=False
    )
```

```python
import functools

import ml_dtypes
import numpy as np
import jax
import jax.numpy as jnp
from jax import lax
from jax.experimental import pallas as pl
from jax.experimental.pallas import tpu as pltpu
from jax.sharding import PartitionSpec as P

TILE = 256
HALF = 128
GROUPS = HALF // 8
CODED = HALF + 8
MESH = pl.DeviceIdType.MESH
F32 = jnp.float32
BF16 = jnp.bfloat16


def dft_tables():
    n = np.arange(HALF)
    out = []
    for odd in (0, 1):
        angle = 2.0 * np.pi * (((2 * n[:, None] + odd) * n[None, :]) % TILE) / TILE
        c, s = np.cos(angle) / 16.0, np.sin(angle) / 16.0
        m = np.block([[c, s], [-s, c]])
        for a in (m, m.T):
            head = a.astype(ml_dtypes.bfloat16)
            out += [head, (a - head.astype(np.float64)).astype(ml_dtypes.bfloat16)]
    return np.stack(out)


def row_twiddles():
    n = 2.0 * np.pi * np.arange(HALF) / TILE
    both = np.stack([np.cos(n), np.sin(n)])
    return np.broadcast_to(both[:, :, None], (2, HALF, HALF)).astype(np.float32)


def halves(x):
    head = x.astype(BF16)
    return head, (x - head.astype(F32)).astype(BF16)


def conj_times(ar, ai, br, bi):
    return ar * br + ai * bi, ar * bi - ai * br


def spread(x):
    return jnp.concatenate([x] * GROUPS, axis=0)


def coded(re, im):
    top = jnp.maximum(jnp.abs(re), jnp.abs(im))
    parts = [top[8 * g : 8 * g + 8] for g in range(GROUPS)]
    while len(parts) > 1:
        parts = [jnp.maximum(a, b) for a, b in zip(parts[::2], parts[1::2])]
    steps = (jnp.log2(jnp.maximum(parts[0], 1e-33)) * 8.0).astype(jnp.int32) + 2
    unit = spread(32767.0 / jnp.exp2(steps.astype(F32) * 0.125))
    high = (re * unit + 32768.5).astype(jnp.int32)
    low = (im * unit + 32768.5).astype(jnp.int32)
    return jnp.concatenate([(high << 16) | low, steps], axis=0)


def decoded(words, weight=1.0 / 32767.0):
    unit = spread(jnp.exp2(words[HALF:].astype(F32) * 0.125) * weight)
    body = words[:HALF]
    high = ((body >> 16) & 65535).astype(F32) - 32768.0
    low = (body & 65535).astype(F32) - 32768.0
    return high * unit, low * unit


def dot(a, b):
    return jnp.dot(a, b, preferred_element_type=F32)


def kernel(
    sizes,
    t_hbm,
    inc_hbm,
    exit_hbm,
    phase_hbm,
    m_hbm,
    rows_hbm,
    anchor_ref,
    live_ref,
    own,
    t_own,
    t_alt,
    t_eff,
    inc,
    exit_v,
    phase,
    rot,
    m_v,
    rows_v,
    waves,
    middle,
    words_in,
    words_out,
    g_alt,
    g_out,
    g_in,
    load_sem,
    t_send,
    t_recv,
    w_send,
    w_recv,
    g_send,
    g_recv,
    go,
):
    n_depth, n_sx, n_sy = sizes
    d, sx, sy = lax.axis_index("depth"), lax.axis_index("sx"), lax.axis_index("sy")
    last = n_depth - 1

    def at(dx, dy):
        return (d, lax.rem(sx + dx + n_sx, n_sx), lax.rem(sy + dy + n_sy, n_sy))

    around = [(i, j) for i in (-1, 0, 1) for j in (-1, 0, 1) if (i, j) != (0, 0)]

    loads = [
        pltpu.make_async_copy(src, dst, load_sem.at[i])
        for i, (src, dst) in enumerate(
            [
                (phase_hbm, phase),
                (m_hbm, m_v),
                (rows_hbm, rows_v),
                (exit_hbm, exit_v),
                (inc_hbm, inc),
                (t_hbm, t_own),
            ]
        )
    ]
    for c in loads:
        c.start()

    barrier = pltpu.get_barrier_semaphore()
    for i, j in around:
        pl.semaphore_signal(barrier, inc=1, device_id=at(i, j), device_id_type=MESH)

    for step in (1, last):
        near = (lax.rem(d + step, n_depth), sx, sy)
        pl.semaphore_signal(barrier, inc=1, device_id=near, device_id_type=MESH)
    pl.semaphore_wait(barrier, len(around) + 2)

    full = pl.ds(0, TILE)
    part = [pl.ds(0, HALF), pl.ds(HALF, HALF)]
    toward = [-1, 1]
    pieces = (
        [(0, part[p], full, (toward[p], 0)) for p in (0, 1)]
        + [(1, full, part[q], (0, toward[q])) for q in (0, 1)]
        + [(2, part[p], part[q], (toward[p], toward[q])) for p in (0, 1) for q in (0, 1)]
    )

    both = pl.ds(0, 2)
    one = [pl.ds(0, 1), pl.ds(1, 1)]
    blocks = (
        [(0, (one[p], both), (toward[p], 0)) for p in (0, 1)]
        + [(1, (both, one[q]), (0, toward[q])) for q in (0, 1)]
        + [(2, (one[p], one[q]), (toward[p], toward[q])) for p in (0, 1) for q in (0, 1)]
    )

    def t_copies(li):
        return [
            pltpu.make_async_remote_copy(
                src_ref=t_hbm.at[li, :, rows, lanes],
                dst_ref=t_alt.at[li, kind, :, rows, lanes],
                send_sem=t_send.at[li * 8 + i],
                recv_sem=t_recv.at[li * 8 + i],
                device_id=at(*way),
                device_id_type=MESH,
            )
            for i, (kind, rows, lanes, way) in enumerate(pieces)
        ]

    def g_copies(li):
        return [
            pltpu.make_async_remote_copy(
                src_ref=g_out.at[li, kind, block[0], block[1]],
                dst_ref=g_in.at[li, kind, block[0], block[1]],
                send_sem=g_send.at[li * 8 + i],
                recv_sem=g_recv.at[li * 8 + i],
                device_id=at(-way[0], -way[1]),
                device_id_type=MESH,
            )
            for i, (kind, block, way) in enumerate(blocks)
        ]

    def w_copy(slot, h):
        return pltpu.make_async_remote_copy(
            src_ref=words_out.at[slot, h],
            dst_ref=words_in.at[slot, h],
            send_sem=w_send.at[slot * 2 + h],
            recv_sem=w_recv.at[slot * 2 + h],
            device_id=(lax.rem(d + last, n_depth), sx, sy),
            device_id_type=MESH,
        )

    odd = lax.rem(d, 2) == 1

    def share():
        for li in (1, 0):
            for c in t_copies(li):
                c.start()

    @pl.when(odd)
    def _():
        share()

    def offsets(slot):
        return anchor_ref[slot, 0] - sx * TILE, anchor_ref[slot, 1] - sy * TILE

    quads = [(0, 0), (0, 1), (1, 0), (1, 1)]

    def masks(slot, p, q):
        out = []
        for a, half, dim in zip(offsets(slot), (p, q), (0, 1)):
            k = lax.broadcasted_iota(jnp.int32, (HALF, HALF), dim)
            out.append(k >= a if half == 0 else k < a + HALF)
        return out

    def rolled(slot, fields):
        ax, ay = offsets(slot)
        i = lax.broadcasted_iota(jnp.int32, (TILE, TILE), 0)
        j = lax.broadcasted_iota(jnp.int32, (TILE, TILE), 1)
        by_rows = jnp.where(((j + ax - i) & (TILE - 1)) == 0, 1.0, 0.0).astype(BF16)
        by_lanes = jnp.where(((i + ay - j) & (TILE - 1)) == 0, 1.0, 0.0).astype(BF16)
        return [dot(by_rows, dot(f, by_lanes).astype(BF16)) for f in fields]

    for c in loads[:5]:
        c.wait()

    @pl.when(d == last)
    def _():
        for slot in (0, 1):
            alive = jnp.where(slot < live_ref[0, 0], 1.0, 0.0).astype(F32)
            for k, f in enumerate(rolled(slot, [exit_v[slot, 0], exit_v[slot, 1]])):
                for h in (0, 1):
                    waves[slot, h, k] = f[h * HALF : (h + 1) * HALF] * alive

    i = lax.broadcasted_iota(jnp.int32, (TILE, TILE), 0)
    j = lax.broadcasted_iota(jnp.int32, (TILE, TILE), 1)
    deal = jnp.where(i == jnp.where(j < HALF, 2 * j, 2 * j - (TILE - 1)), 1.0, 0.0).astype(BF16)
    deal_rows = jnp.where(j == jnp.where(i < HALF, 2 * i, 2 * i - (TILE - 1)), 1.0, 0.0).astype(BF16)
    p = phase[...]
    p0 = p.astype(BF16)
    p1, p2 = halves(p - p0.astype(F32))
    f0, f1, f2 = [dot(deal_rows, dot(q, deal).astype(BF16)) for q in (p0, p1, p2)]
    phase[...] = (f0 + f1) + f2
    for h in (0, 1):
        ordered = phase[part[h], :]
        for k, f in enumerate((jnp.cos(ordered), jnp.sin(ordered))):
            for g in (0, 1):
                rot[k, g, :, part[h]] = f[:, g * HALF : (g + 1) * HALF]

    def roll_incident(slot):
        got = rolled(slot, [inc[li, slot, k] for li in (0, 1) for k in (0, 1)])
        for n, f in enumerate(got):
            inc[n // 2, slot, n % 2] = f.astype(BF16)

    for slot in (0, 1):
        roll_incident(slot)

    zero = jnp.zeros((HALF, HALF), F32)

    def window(li, slot):
        for p, q in quads:
            on_x, on_y = masks(slot, p, q)
            spot = (part[p], part[q])
            for k in (0, 1):
                here = t_own[(li, k) + spot].astype(F32)
                tx, ty, txy = [t_alt[(li, kind, k) + spot].astype(F32) for kind in range(3)]
                t_eff[(li, slot, k) + spot] = jnp.where(
                    on_x, jnp.where(on_y, here, ty), jnp.where(on_y, tx, txy)
                ).astype(BF16)

    def border(li):
        for p in (0, 1):
            edge_x, edge_y = [(n - 1, 0)[p] for n in (n_sx, n_sy)]

            @pl.when(sx == edge_x)
            def _(p=p):
                for kind in (0, 2):
                    t_alt[li, kind, :, part[p], :] = jnp.zeros((2, HALF, TILE), BF16)

            @pl.when(sy == edge_y)
            def _(p=p):
                for kind in (1, 2):
                    t_alt[li, kind, :, :, part[p]] = jnp.zeros((2, TILE, HALF), BF16)

    def windows(li):
        for c in t_copies(li)[1 if li == 1 else 0 :]:
            c.wait_recv()
        border(li)
        for slot in (0, 1):
            window(li, slot)

    def beside(a, b):
        return jnp.concatenate([a, b], axis=1)

    def above(a, b):
        return jnp.concatenate([a, b], axis=0)

    def right(z, first):
        head, tail = halves(z)
        table = jnp.concatenate([m_v[first], m_v[first], m_v[first + 1]], axis=0)
        rows = jnp.concatenate([head, tail, head], axis=1)
        parts = []
        for r in (slice(0, HALF), slice(HALF, 2 * HALF)):
            two = dot(above(head[r], tail[r]), m_v[first])
            parts.append((two[:HALF] + two[HALF:]) + dot(head[r], m_v[first + 1]))
        return above(*parts)

    def left(z, first):
        head, tail = halves(z)
        table = jnp.concatenate([m_v[first], m_v[first + 1], m_v[first]], axis=1)
        cols = jnp.concatenate([head, head, tail], axis=0)
        parts = []
        for r in (slice(0, HALF), slice(HALF, 2 * HALF)):
            two = dot(above(m_v[first, r], m_v[first + 1, r]), head)
            parts.append((two[:HALF] + two[HALF:]) + dot(m_v[first, r], tail))
        return above(*parts)

    c, s = rows_v[0], rows_v[1]

    def between(y):
        a, b = y[:HALF], y[HALF:]
        sm, df = a + b, a - b
        dr, di = df[:, :HALF], df[:, HALF:]
        return above(beside(sm[:, :HALF], dr * c + di * s), beside(sm[:, HALF:], di * c - dr * s))

    def turned(g, x):
        xr, xi = x[:HALF], x[HALF:]
        cp, sp = rot[0, g], rot[1, g]
        return above(xr * cp + xi * sp, xi * cp - xr * sp)

    def undealt(e):
        er, ei = e[:HALF, HALF:], e[HALF:, HALF:]
        tr, ti = er * c - ei * s, ei * c + er * s
        vr, vi = e[:HALF, :HALF], e[HALF:, :HALF]
        return above(beside(vr + tr, vi + ti), beside(vr - tr, vi - ti))

    def finish(joined, store):
        for h in (0, 1):
            e, o = [j[h * HALF : (h + 1) * HALF] for j in joined]
            low, high = e + o, e - o
            store(h, low[:, :HALF], high[:, :HALF], low[:, HALF:], high[:, HALF:])

    def propagated(fields):
        a = [beside(re[:, :HALF], im[:, :HALF]) for re, im in fields]
        b = [beside(re[:, HALF:], im[:, HALF:]) for re, im in fields]
        z0 = above(a[0] + b[0], a[1] + b[1])
        z1 = above(a[0] - b[0], a[1] - b[1])

        y0 = right(z0, 2)
        y1 = right(z1, 6)
        x0 = left(between(y0), 0)
        x1 = left(between(y1), 0)
        e0 = left(turned(0, x0), 2)
        e1 = left(turned(1, x1), 2)
        return [right(undealt(e0), 0), right(undealt(e1), 4)]

    def through(li, slot, h, re, im):
        rows = part[h]
        tr = t_eff[li, slot, 0, rows, :].astype(F32)
        ti = t_eff[li, slot, 1, rows, :].astype(F32)
        return conj_times(tr, ti, re, im)

    def shares(li, slot, p, q):
        wave = waves if li == 1 else middle
        er = inc[li, slot, 0, part[p], part[q]].astype(F32)
        ei = inc[li, slot, 1, part[p], part[q]].astype(F32)
        on_x, on_y = masks(slot, p, q)
        out = []
        for t in conj_times(er, ei, wave[slot, p, 0, :, part[q]], wave[slot, p, 1, :, part[q]]):
            inside = jnp.where(on_x, t, zero)
            beyond = jnp.where(on_x, zero, t)
            out.append(
                [
                    jnp.where(on_y, inside, zero),
                    jnp.where(on_y, beyond, zero),
                    jnp.where(on_y, zero, inside),
                    jnp.where(on_y, zero, beyond),
                ]
            )
        return out

    def first_gradient(li):
        for p, q in quads:
            spot = (part[p], part[q])
            for k, t in enumerate(shares(li, 0, p, q)):
                own[(li, k) + spot] = t[0]
                for kind in range(3):
                    g_alt[(li, kind, k) + spot] = t[kind + 1]

    def second_gradient(li):
        copies = g_copies(li)
        for p, q in quads:
            spot = (part[p], part[q])
            re, im = shares(li, 1, p, q)
            for kind in (2, 0, 1):
                g_out[li, kind, p, q] = coded(
                    g_alt[(li, kind, 0) + spot] + re[kind + 1], g_alt[(li, kind, 1) + spot] + im[kind + 1]
                )
            copies[4 + 2 * p + q].start()
            if q == 1:
                copies[p].start()
            if p == 1:
                copies[2 + q].start()
            own[(li, 0) + spot] += re[0]
            own[(li, 1) + spot] += im[0]

    def gradient(li, slot):
        @pl.when(slot == 0)
        def _():
            first_gradient(li)

        @pl.when(slot == 1)
        def _():
            second_gradient(li)

    def apply_layer(li, slot, source, store):
        fields = [through(li, slot, h, source[slot, h, 0], source[slot, h, 1]) for h in (0, 1)]
        finish(propagated(fields), store)

    loads[5].wait()

    @pl.when(odd)
    def _():
        t_copies(1)[0].wait_recv()
        pl.semaphore_signal(go, inc=1, device_id=(d - 1, sx, sy), device_id_type=MESH)

    @pl.when(jnp.logical_not(odd))
    def _():
        pl.semaphore_wait(go, 1)
        share()
        t_copies(1)[0].wait_recv()

    windows(1)

    early = d < 2

    def one_slot(slot, carry):
        @pl.when(d < last)
        def _():
            for h in (0, 1):
                w_copy(slot, h).wait_recv()
                for q in (0, 1):
                    re, im = decoded(words_in[slot, h, q])
                    waves[slot, h, 0, :, part[q]] = re
                    waves[slot, h, 1, :, part[q]] = im

        @pl.when(early)
        def _():
            gradient(1, slot)

        def keep(h, lr, hr, li_, hi_):
            middle[slot, h, 0, :, :HALF] = lr
            middle[slot, h, 0, :, HALF:] = hr
            middle[slot, h, 1, :, :HALF] = li_
            middle[slot, h, 1, :, HALF:] = hi_

        apply_layer(1, slot, waves, keep)

        @pl.when(slot == 0)
        def _():
            windows(0)

        @pl.when(early)
        def _():
            gradient(0, slot)

        @pl.when(d > 0)
        def _():
            def encode(h, lr, hr, li_, hi_):
                words_out[slot, h, 0] = coded(lr, li_)
                words_out[slot, h, 1] = coded(hr, hi_)
                w_copy(slot, h).start()

            apply_layer(0, slot, middle, encode)

        return carry

    lax.fori_loop(0, 2, one_slot, 0)

    @pl.when(jnp.logical_not(early))
    def _():
        for li in (1, 0):
            first_gradient(li)
            second_gradient(li)

    for li in (1, 0):
        for c in t_copies(li):
            c.wait_send()

    @pl.when(d > 0)
    def _():
        for slot in (0, 1):
            for h in (0, 1):
                w_copy(slot, h).wait_send()

    from_x = [jnp.where(sx > 0, 1.0, 0.0), jnp.where(sx < n_sx - 1, 1.0, 0.0)]
    from_y = [jnp.where(sy > 0, 1.0, 0.0), jnp.where(sy < n_sy - 1, 1.0, 0.0)]
    for li in (1, 0):
        copies = g_copies(li)
        for p, q in quads:
            if q == 0:
                copies[p].wait_recv()
            if p == 0:
                copies[2 + q].wait_recv()
            copies[4 + 2 * p + q].wait_recv()
            weights = (from_x[p], from_y[q], from_x[p] * from_y[q])
            got = [decoded(g_in[li, kind, p, q], weights[kind] / 32767.0) for kind in range(3)]
            for k in (0, 1):
                own[li, k, part[p], part[q]] += (got[0][k] + got[1][k]) + got[2][k]

    for li in (1, 0):
        for c in g_copies(li):
            c.wait_send()


def shards(transmission, incident, exit_adjoint, propagator_phase, scan_anchor, live_count):
    sizes = tuple(lax.axis_size(a) for a in ("depth", "sx", "sy"))
    slab = transmission.shape[0]
    any_space = pl.BlockSpec(memory_space=pl.ANY)
    smem = pl.BlockSpec(memory_space=pltpu.SMEM)
    plane = (TILE, TILE)
    dma = pltpu.SemaphoreType.DMA
    return pl.pallas_call(
        functools.partial(kernel, sizes),
        out_shape=pltpu.VMEM(transmission.shape, F32),
        in_specs=[any_space] * 6 + [smem, smem],
        out_specs=pl.BlockSpec(memory_space=pltpu.VMEM),
        scratch_shapes=[
            pltpu.VMEM((slab, 2) + plane, BF16),
            pltpu.VMEM((slab, 3, 2) + plane, BF16),
            pltpu.VMEM((slab, 2, 2) + plane, BF16),
            pltpu.VMEM((slab, 2, 2) + plane, BF16),
            pltpu.VMEM((2, 2) + plane, BF16),
            pltpu.VMEM(plane, F32),
            pltpu.VMEM((2, 2, HALF, TILE), F32),
            pltpu.VMEM((8,) + plane, BF16),
            pltpu.VMEM((2, HALF, HALF), F32),
            pltpu.VMEM((2, 2, 2, HALF, TILE), F32),
            pltpu.VMEM((2, 2, 2, HALF, TILE), F32),
            pltpu.VMEM((2, 2, 2, CODED, HALF), jnp.int32),
            pltpu.VMEM((2, 2, 2, CODED, HALF), jnp.int32),
            pltpu.VMEM((slab, 3, 2) + plane, F32),
            pltpu.VMEM((slab, 3, 2, 2, CODED, HALF), jnp.int32),
            pltpu.VMEM((slab, 3, 2, 2, CODED, HALF), jnp.int32),
            dma((6,)),
            dma((16,)),
            dma((16,)),
            dma((4,)),
            dma((4,)),
            dma((16,)),
            dma((16,)),
            pltpu.SemaphoreType.REGULAR,
        ],
        compiler_params=pltpu.CompilerParams(
            collective_id=0, has_side_effects=True, vmem_limit_bytes=60 * 1024 * 1024
        ),
    )(
        transmission,
        incident,
        exit_adjoint,
        propagator_phase,
        jnp.asarray(dft_tables()),
        jnp.asarray(row_twiddles()),
        scan_anchor,
        live_count[None],
    )


def solution(mesh):
    placed = (
        P("depth", None, "sx", "sy"),
        P("depth", ("sx", "sy"), None, None, None),
        P(("sx", "sy"), None, None, None),
        P(),
        P(("sx", "sy"), None),
        P(("sx", "sy")),
    )
    return jax.shard_map(
        shards, mesh=mesh, in_specs=placed, out_specs=P("depth", None, "sx", "sy"), check_vma=False
    )
```

```python
import functools

import ml_dtypes
import numpy as np
import jax
import jax.numpy as jnp
from jax import lax
from jax.experimental import pallas as pl
from jax.experimental.pallas import tpu as pltpu
from jax.sharding import PartitionSpec as P

TILE = 256
HALF = 128
GROUPS = HALF // 8
CODED = HALF + 8
MESH = pl.DeviceIdType.MESH
F32 = jnp.float32
BF16 = jnp.bfloat16


def dft_tables():
    n = np.arange(HALF)
    out = []
    for odd in (0, 1):
        angle = 2.0 * np.pi * (((2 * n[:, None] + odd) * n[None, :]) % TILE) / TILE
        c, s = np.cos(angle) / 16.0, np.sin(angle) / 16.0
        m = np.block([[c, s], [-s, c]])
        for a in (m, m.T):
            head = a.astype(ml_dtypes.bfloat16)
            out += [head, (a - head.astype(np.float64)).astype(ml_dtypes.bfloat16)]
    return np.stack(out)


def row_twiddles():
    n = 2.0 * np.pi * np.arange(HALF) / TILE
    both = np.stack([np.cos(n), np.sin(n)])
    return np.broadcast_to(both[:, :, None], (2, HALF, HALF)).astype(np.float32)


def halves(x):
    head = x.astype(BF16)
    return head, (x - head.astype(F32)).astype(BF16)


def conj_times(ar, ai, br, bi):
    return ar * br + ai * bi, ar * bi - ai * br


def spread(x):
    return jnp.concatenate([x] * GROUPS, axis=0)


def coded(re, im):
    top = jnp.maximum(jnp.abs(re), jnp.abs(im))
    parts = [top[8 * g : 8 * g + 8] for g in range(GROUPS)]
    while len(parts) > 1:
        parts = [jnp.maximum(a, b) for a, b in zip(parts[::2], parts[1::2])]
    steps = (jnp.log2(jnp.maximum(parts[0], 1e-33)) * 8.0).astype(jnp.int32) + 2
    unit = spread(32767.0 / jnp.exp2(steps.astype(F32) * 0.125))
    high = (re * unit + 32768.5).astype(jnp.int32)
    low = (im * unit + 32768.5).astype(jnp.int32)
    return jnp.concatenate([(high << 16) | low, steps], axis=0)


def decoded(words, weight=1.0 / 32767.0):
    unit = spread(jnp.exp2(words[HALF:].astype(F32) * 0.125) * weight)
    body = words[:HALF]
    high = ((body >> 16) & 65535).astype(F32) - 32768.0
    low = (body & 65535).astype(F32) - 32768.0
    return high * unit, low * unit


def dot(a, b):
    return jnp.dot(a, b, preferred_element_type=F32)


def kernel(
    sizes,
    t_hbm,
    inc_hbm,
    exit_hbm,
    phase_hbm,
    m_hbm,
    rows_hbm,
    anchor_hbm,
    live_hbm,
    own,
    t_own,
    t_alt,
    t_eff,
    inc,
    exit_v,
    phase,
    rot,
    m_v,
    rows_v,
    waves,
    middle,
    words_in,
    words_out,
    g_alt,
    g_out,
    g_in,
    load_sem,
    t_send,
    t_recv,
    w_send,
    w_recv,
    g_send,
    g_recv,
    go,
    anchor_ref,
    live_ref,
):
    n_depth, n_sx, n_sy = sizes
    d, sx, sy = lax.axis_index("depth"), lax.axis_index("sx"), lax.axis_index("sy")
    last = n_depth - 1

    def at(dx, dy):
        return (d, lax.rem(sx + dx + n_sx, n_sx), lax.rem(sy + dy + n_sy, n_sy))

    around = [(i, j) for i in (-1, 0, 1) for j in (-1, 0, 1) if (i, j) != (0, 0)]

    barrier = pltpu.get_barrier_semaphore()
    for i, j in around:
        pl.semaphore_signal(barrier, inc=1, device_id=at(i, j), device_id_type=MESH)


    @pl.when(d > 0)
    def _():
        pl.semaphore_signal(barrier, inc=1, device_id=(d - 1, sx, sy), device_id_type=MESH)

    @pl.when(d < last)
    def _():
        pl.semaphore_signal(barrier, inc=1, device_id=(d + 1, sx, sy), device_id_type=MESH)

    loads = [
        pltpu.make_async_copy(src, dst, load_sem.at[i])
        for i, (src, dst) in enumerate(
            [
                (phase_hbm, phase),
                (m_hbm, m_v),
                (rows_hbm, rows_v),
                (exit_hbm, exit_v),
                (inc_hbm, inc),
                (t_hbm, t_own),
                (anchor_hbm, anchor_ref),
                (live_hbm, live_ref),
            ]
        )
    ]
    for c in loads:
        c.start()

    ends = jnp.where(d > 0, 1, 0) + jnp.where(d < last, 1, 0)
    pl.semaphore_wait(barrier, len(around) + ends)

    full = pl.ds(0, TILE)
    part = [pl.ds(0, HALF), pl.ds(HALF, HALF)]
    toward = [-1, 1]
    pieces = (
        [(0, part[p], full, (toward[p], 0)) for p in (0, 1)]
        + [(1, full, part[q], (0, toward[q])) for q in (0, 1)]
        + [(2, part[p], part[q], (toward[p], toward[q])) for p in (0, 1) for q in (0, 1)]
    )

    both = pl.ds(0, 2)
    one = [pl.ds(0, 1), pl.ds(1, 1)]
    blocks = (
        [(0, (one[p], both), (toward[p], 0)) for p in (0, 1)]
        + [(1, (both, one[q]), (0, toward[q])) for q in (0, 1)]
        + [(2, (one[p], one[q]), (toward[p], toward[q])) for p in (0, 1) for q in (0, 1)]
    )

    def t_copies(li):
        return [
            pltpu.make_async_remote_copy(
                src_ref=t_hbm.at[li, :, rows, lanes],
                dst_ref=t_alt.at[li, kind, :, rows, lanes],
                send_sem=t_send.at[li * 8 + i],
                recv_sem=t_recv.at[li * 8 + i],
                device_id=at(*way),
                device_id_type=MESH,
            )
            for i, (kind, rows, lanes, way) in enumerate(pieces)
        ]

    def g_copies(li):
        return [
            pltpu.make_async_remote_copy(
                src_ref=g_out.at[li, kind, block[0], block[1]],
                dst_ref=g_in.at[li, kind, block[0], block[1]],
                send_sem=g_send.at[li * 8 + i],
                recv_sem=g_recv.at[li * 8 + i],
                device_id=at(-way[0], -way[1]),
                device_id_type=MESH,
            )
            for i, (kind, block, way) in enumerate(blocks)
        ]

    def w_copy(slot, h):
        return pltpu.make_async_remote_copy(
            src_ref=words_out.at[slot, h],
            dst_ref=words_in.at[slot, h],
            send_sem=w_send.at[slot * 2 + h],
            recv_sem=w_recv.at[slot * 2 + h],
            device_id=(lax.rem(d + last, n_depth), sx, sy),
            device_id_type=MESH,
        )

    odd = lax.rem(d, 2) == 1

    def share():
        for li in (1, 0):
            for c in reversed(t_copies(li)):
                c.start()

    @pl.when(odd)
    def _():
        share()

    def offsets(slot):
        return anchor_ref[slot, 0] - sx * TILE, anchor_ref[slot, 1] - sy * TILE

    quads = [(0, 0), (0, 1), (1, 0), (1, 1)]

    def masks(slot, p, q):
        out = []
        for a, half, dim in zip(offsets(slot), (p, q), (0, 1)):
            k = lax.broadcasted_iota(jnp.int32, (HALF, HALF), dim)
            out.append(k >= a if half == 0 else k < a + HALF)
        return out

    def rolled(slot, fields):
        ax, ay = offsets(slot)
        i = lax.broadcasted_iota(jnp.int32, (TILE, TILE), 0)
        j = lax.broadcasted_iota(jnp.int32, (TILE, TILE), 1)
        by_rows = jnp.where(((j + ax - i) & (TILE - 1)) == 0, 1.0, 0.0).astype(BF16)
        by_lanes = jnp.where(((i + ay - j) & (TILE - 1)) == 0, 1.0, 0.0).astype(BF16)
        return [dot(by_rows, dot(f, by_lanes).astype(BF16)) for f in fields]

    for c in loads:
        c.wait()

    @pl.when(d == last)
    def _():
        for slot in (0, 1):
            alive = jnp.where(slot < live_ref[0], 1.0, 0.0).astype(F32)
            for k, f in enumerate(rolled(slot, [exit_v[slot, 0], exit_v[slot, 1]])):
                for h in (0, 1):
                    waves[slot, h, k] = f[h * HALF : (h + 1) * HALF] * alive

    i = lax.broadcasted_iota(jnp.int32, (TILE, TILE), 0)
    j = lax.broadcasted_iota(jnp.int32, (TILE, TILE), 1)
    deal = jnp.where(i == jnp.where(j < HALF, 2 * j, 2 * j - (TILE - 1)), 1.0, 0.0).astype(BF16)
    deal_rows = jnp.where(j == jnp.where(i < HALF, 2 * i, 2 * i - (TILE - 1)), 1.0, 0.0).astype(BF16)
    p = phase[...]
    p0 = p.astype(BF16)
    p1, p2 = halves(p - p0.astype(F32))
    f0, f1, f2 = [dot(deal_rows, dot(q, deal).astype(BF16)) for q in (p0, p1, p2)]
    phase[...] = (f0 + f1) + f2
    for h in (0, 1):
        ordered = phase[part[h], :]
        for k, f in enumerate((jnp.cos(ordered), jnp.sin(ordered))):
            for g in (0, 1):
                rot[k, g, :, part[h]] = f[:, g * HALF : (g + 1) * HALF]

    def roll_incident(slot):
        got = rolled(slot, [inc[li, slot, k] for li in (0, 1) for k in (0, 1)])
        for n, f in enumerate(got):
            inc[n // 2, slot, n % 2] = f.astype(BF16)

    for slot in (0, 1):
        roll_incident(slot)

    zero = jnp.zeros((HALF, HALF), F32)

    def window(li, slot):
        for p, q in quads:
            on_x, on_y = masks(slot, p, q)
            spot = (part[p], part[q])
            for k in (0, 1):
                here = t_own[(li, k) + spot].astype(F32)
                tx, ty, txy = [t_alt[(li, kind, k) + spot].astype(F32) for kind in range(3)]
                t_eff[(li, slot, k) + spot] = jnp.where(
                    on_x, jnp.where(on_y, here, ty), jnp.where(on_y, tx, txy)
                ).astype(BF16)

    def border(li):
        for p in (0, 1):
            edge_x, edge_y = [(n - 1, 0)[p] for n in (n_sx, n_sy)]

            @pl.when(sx == edge_x)
            def _(p=p):
                for kind in (0, 2):
                    t_alt[li, kind, :, part[p], :] = jnp.zeros((2, HALF, TILE), BF16)

            @pl.when(sy == edge_y)
            def _(p=p):
                for kind in (1, 2):
                    t_alt[li, kind, :, :, part[p]] = jnp.zeros((2, TILE, HALF), BF16)

    def windows(li):
        for c in t_copies(li)[1 if li == 1 else 0 :]:
            c.wait_recv()
        border(li)
        for slot in (0, 1):
            window(li, slot)

    def beside(a, b):
        return jnp.concatenate([a, b], axis=1)

    def above(a, b):
        return jnp.concatenate([a, b], axis=0)

    def right(z, first):
        head, tail = halves(z)
        table = jnp.concatenate([m_v[first], m_v[first], m_v[first + 1]], axis=0)
        rows = jnp.concatenate([head, tail, head], axis=1)
        parts = []
        for r in (slice(0, HALF), slice(HALF, 2 * HALF)):
            two = dot(above(head[r], tail[r]), m_v[first])
            parts.append((two[:HALF] + two[HALF:]) + dot(head[r], m_v[first + 1]))
        return above(*parts)

    def left(z, first):
        head, tail = halves(z)
        table = jnp.concatenate([m_v[first], m_v[first + 1], m_v[first]], axis=1)
        cols = jnp.concatenate([head, head, tail], axis=0)
        parts = []
        for r in (slice(0, HALF), slice(HALF, 2 * HALF)):
            two = dot(above(m_v[first, r], m_v[first + 1, r]), head)
            parts.append((two[:HALF] + two[HALF:]) + dot(m_v[first, r], tail))
        return above(*parts)

    c, s = rows_v[0], rows_v[1]

    def between(y):
        a, b = y[:HALF], y[HALF:]
        sm, df = a + b, a - b
        dr, di = df[:, :HALF], df[:, HALF:]
        return above(beside(sm[:, :HALF], dr * c + di * s), beside(sm[:, HALF:], di * c - dr * s))

    def turned(g, x):
        xr, xi = x[:HALF], x[HALF:]
        cp, sp = rot[0, g], rot[1, g]
        return above(xr * cp + xi * sp, xi * cp - xr * sp)

    def undealt(e):
        er, ei = e[:HALF, HALF:], e[HALF:, HALF:]
        tr, ti = er * c - ei * s, ei * c + er * s
        vr, vi = e[:HALF, :HALF], e[HALF:, :HALF]
        return above(beside(vr + tr, vi + ti), beside(vr - tr, vi - ti))

    def finish(joined, store):
        for h in (0, 1):
            e, o = [j[h * HALF : (h + 1) * HALF] for j in joined]
            low, high = e + o, e - o
            store(h, low[:, :HALF], high[:, :HALF], low[:, HALF:], high[:, HALF:])

    def propagated(fields):
        a = [beside(re[:, :HALF], im[:, :HALF]) for re, im in fields]
        b = [beside(re[:, HALF:], im[:, HALF:]) for re, im in fields]
        z0 = above(a[0] + b[0], a[1] + b[1])
        z1 = above(a[0] - b[0], a[1] - b[1])

        y0 = right(z0, 2)
        y1 = right(z1, 6)
        x0 = left(between(y0), 0)
        x1 = left(between(y1), 0)
        e0 = left(turned(0, x0), 2)
        e1 = left(turned(1, x1), 2)
        return [right(undealt(e0), 0), right(undealt(e1), 4)]

    def through(li, slot, h, re, im):
        rows = part[h]
        tr = t_eff[li, slot, 0, rows, :].astype(F32)
        ti = t_eff[li, slot, 1, rows, :].astype(F32)
        return conj_times(tr, ti, re, im)

    def shares(li, slot, p, q):
        wave = waves if li == 1 else middle
        er = inc[li, slot, 0, part[p], part[q]].astype(F32)
        ei = inc[li, slot, 1, part[p], part[q]].astype(F32)
        on_x, on_y = masks(slot, p, q)
        out = []
        for t in conj_times(er, ei, wave[slot, p, 0, :, part[q]], wave[slot, p, 1, :, part[q]]):
            inside = jnp.where(on_x, t, zero)
            beyond = jnp.where(on_x, zero, t)
            out.append(
                [
                    jnp.where(on_y, inside, zero),
                    jnp.where(on_y, beyond, zero),
                    jnp.where(on_y, zero, inside),
                    jnp.where(on_y, zero, beyond),
                ]
            )
        return out

    def first_gradient(li):
        for p, q in quads:
            spot = (part[p], part[q])
            for k, t in enumerate(shares(li, 0, p, q)):
                own[(li, k) + spot] = t[0]
                for kind in range(3):
                    g_alt[(li, kind, k) + spot] = t[kind + 1]

    def second_gradient(li):
        copies = g_copies(li)
        for p, q in quads:
            spot = (part[p], part[q])
            re, im = shares(li, 1, p, q)
            for kind in (2, 0, 1):
                g_out[li, kind, p, q] = coded(
                    g_alt[(li, kind, 0) + spot] + re[kind + 1], g_alt[(li, kind, 1) + spot] + im[kind + 1]
                )
            copies[4 + 2 * p + q].start()
            if q == 1:
                copies[p].start()
            if p == 1:
                copies[2 + q].start()
            own[(li, 0) + spot] += re[0]
            own[(li, 1) + spot] += im[0]

    def gradient(li, slot):
        @pl.when(slot == 0)
        def _():
            first_gradient(li)

        @pl.when(slot == 1)
        def _():
            second_gradient(li)

    def apply_layer(li, slot, source, store):
        fields = [through(li, slot, h, source[slot, h, 0], source[slot, h, 1]) for h in (0, 1)]
        finish(propagated(fields), store)

    @pl.when(odd)
    def _():
        t_copies(1)[0].wait_recv()
        pl.semaphore_signal(go, inc=1, device_id=(d - 1, sx, sy), device_id_type=MESH)

    @pl.when(jnp.logical_not(odd))
    def _():
        pl.semaphore_wait(go, 1)
        share()
        t_copies(1)[0].wait_recv()

    windows(1)

    early = d < 2

    def one_slot(slot, carry):
        @pl.when(d < last)
        def _():
            for h in (0, 1):
                w_copy(slot, h).wait_recv()
                for q in (0, 1):
                    re, im = decoded(words_in[slot, h, q])
                    waves[slot, h, 0, :, part[q]] = re
                    waves[slot, h, 1, :, part[q]] = im

        @pl.when(early)
        def _():
            gradient(1, slot)

        def keep(h, lr, hr, li_, hi_):
            middle[slot, h, 0, :, :HALF] = lr
            middle[slot, h, 0, :, HALF:] = hr
            middle[slot, h, 1, :, :HALF] = li_
            middle[slot, h, 1, :, HALF:] = hi_

        apply_layer(1, slot, waves, keep)

        @pl.when(slot == 0)
        def _():
            windows(0)

        @pl.when(early)
        def _():
            gradient(0, slot)

        @pl.when(d > 0)
        def _():
            def encode(h, lr, hr, li_, hi_):
                words_out[slot, h, 0] = coded(lr, li_)
                words_out[slot, h, 1] = coded(hr, hi_)
                w_copy(slot, h).start()

            apply_layer(0, slot, middle, encode)

        return carry

    lax.fori_loop(0, 2, one_slot, 0)

    @pl.when(jnp.logical_not(early))
    def _():
        for li in (1, 0):
            first_gradient(li)
            second_gradient(li)

    for li in (1, 0):
        for c in t_copies(li):
            c.wait_send()

    @pl.when(d > 0)
    def _():
        for slot in (0, 1):
            for h in (0, 1):
                w_copy(slot, h).wait_send()

    from_x = [jnp.where(sx > 0, 1.0, 0.0), jnp.where(sx < n_sx - 1, 1.0, 0.0)]
    from_y = [jnp.where(sy > 0, 1.0, 0.0), jnp.where(sy < n_sy - 1, 1.0, 0.0)]
    for li in (1, 0):
        copies = g_copies(li)
        for p, q in quads:
            if q == 0:
                copies[p].wait_recv()
            if p == 0:
                copies[2 + q].wait_recv()
            copies[4 + 2 * p + q].wait_recv()
            weights = (from_x[p], from_y[q], from_x[p] * from_y[q])
            got = [decoded(g_in[li, kind, p, q], weights[kind] / 32767.0) for kind in range(3)]
            for k in (0, 1):
                own[li, k, part[p], part[q]] += (got[0][k] + got[1][k]) + got[2][k]

    for li in (1, 0):
        for c in g_copies(li):
            c.wait_send()


def shards(transmission, incident, exit_adjoint, propagator_phase, scan_anchor, live_count):
    sizes = tuple(lax.axis_size(a) for a in ("depth", "sx", "sy"))
    slab = transmission.shape[0]
    any_space = pl.BlockSpec(memory_space=pl.ANY)
    plane = (TILE, TILE)
    dma = pltpu.SemaphoreType.DMA
    return pl.pallas_call(
        functools.partial(kernel, sizes),
        out_shape=pltpu.VMEM(transmission.shape, F32),
        in_specs=[any_space] * 8,
        out_specs=pl.BlockSpec(memory_space=pltpu.VMEM),
        scratch_shapes=[
            pltpu.VMEM((slab, 2) + plane, BF16),
            pltpu.VMEM((slab, 3, 2) + plane, BF16),
            pltpu.VMEM((slab, 2, 2) + plane, BF16),
            pltpu.VMEM((slab, 2, 2) + plane, BF16),
            pltpu.VMEM((2, 2) + plane, BF16),
            pltpu.VMEM(plane, F32),
            pltpu.VMEM((2, 2, HALF, TILE), F32),
            pltpu.VMEM((8,) + plane, BF16),
            pltpu.VMEM((2, HALF, HALF), F32),
            pltpu.VMEM((2, 2, 2, HALF, TILE), F32),
            pltpu.VMEM((2, 2, 2, HALF, TILE), F32),
            pltpu.VMEM((2, 2, 2, CODED, HALF), jnp.int32),
            pltpu.VMEM((2, 2, 2, CODED, HALF), jnp.int32),
            pltpu.VMEM((slab, 3, 2) + plane, F32),
            pltpu.VMEM((slab, 3, 2, 2, CODED, HALF), jnp.int32),
            pltpu.VMEM((slab, 3, 2, 2, CODED, HALF), jnp.int32),
            dma((8,)),
            dma((16,)),
            dma((16,)),
            dma((4,)),
            dma((4,)),
            dma((16,)),
            dma((16,)),
            pltpu.SemaphoreType.REGULAR,
            pltpu.SMEM((2, 2), jnp.int32),
            pltpu.SMEM((1,), jnp.int32),
        ],
        compiler_params=pltpu.CompilerParams(
            collective_id=0, has_side_effects=True, vmem_limit_bytes=60 * 1024 * 1024
        ),
    )(
        transmission,
        incident,
        exit_adjoint,
        propagator_phase,
        jnp.asarray(dft_tables()),
        jnp.asarray(row_twiddles()),
        scan_anchor,
        live_count,
    )


def solution(mesh):
    placed = (
        P("depth", None, "sx", "sy"),
        P("depth", ("sx", "sy"), None, None, None),
        P(("sx", "sy"), None, None, None),
        P(),
        P(("sx", "sy"), None),
        P(("sx", "sy")),
    )
    return jax.shard_map(
        shards, mesh=mesh, in_specs=placed, out_specs=P("depth", None, "sx", "sy"), check_vma=False
    )
```

```python
import functools

import ml_dtypes
import numpy as np
import jax
import jax.numpy as jnp
from jax import lax
from jax.experimental import pallas as pl
from jax.experimental.pallas import tpu as pltpu
from jax.sharding import PartitionSpec as P

TILE = 256
HALF = 128
GROUPS = HALF // 8
CODED = HALF + 8
MESH = pl.DeviceIdType.MESH
F32 = jnp.float32
BF16 = jnp.bfloat16


def dft_tables():
    n = np.arange(HALF)
    out = []
    for odd in (0, 1):
        angle = 2.0 * np.pi * (((2 * n[:, None] + odd) * n[None, :]) % TILE) / TILE
        c, s = np.cos(angle) / 16.0, np.sin(angle) / 16.0
        m = np.block([[c, s], [-s, c]])
        for a in (m, m.T):
            head = a.astype(ml_dtypes.bfloat16)
            out += [head, (a - head.astype(np.float64)).astype(ml_dtypes.bfloat16)]
    return np.stack(out)


def row_twiddles():
    n = 2.0 * np.pi * np.arange(HALF) / TILE
    both = np.stack([np.cos(n), np.sin(n)])
    return np.broadcast_to(both[:, :, None], (2, HALF, HALF)).astype(np.float32)


def halves(x):
    head = x.astype(BF16)
    return head, (x - head.astype(F32)).astype(BF16)


def conj_times(ar, ai, br, bi):
    return ar * br + ai * bi, ar * bi - ai * br


def spread(x):
    return jnp.concatenate([x] * GROUPS, axis=0)


def coded(re, im):
    top = jnp.maximum(jnp.abs(re), jnp.abs(im))
    parts = [top[8 * g : 8 * g + 8] for g in range(GROUPS)]
    while len(parts) > 1:
        parts = [jnp.maximum(a, b) for a, b in zip(parts[::2], parts[1::2])]
    steps = (jnp.log2(jnp.maximum(parts[0], 1e-33)) * 8.0).astype(jnp.int32) + 2
    unit = spread(32767.0 / jnp.exp2(steps.astype(F32) * 0.125))
    high = (re * unit + 32768.5).astype(jnp.int32)
    low = (im * unit + 32768.5).astype(jnp.int32)
    return jnp.concatenate([(high << 16) | low, steps], axis=0)


def decoded(words, weight=1.0 / 32767.0):
    unit = spread(jnp.exp2(words[HALF:].astype(F32) * 0.125) * weight)
    body = words[:HALF]
    high = ((body >> 16) & 65535).astype(F32) - 32768.0
    low = (body & 65535).astype(F32) - 32768.0
    return high * unit, low * unit


def dot(a, b):
    return jnp.dot(a, b, preferred_element_type=F32)


def kernel(
    sizes,
    t_hbm,
    inc_hbm,
    exit_hbm,
    phase_hbm,
    m_hbm,
    rows_hbm,
    anchor_hbm,
    live_hbm,
    own,
    t_own,
    t_alt,
    t_eff,
    inc,
    exit_v,
    phase,
    rot,
    m_v,
    rows_v,
    waves,
    middle,
    words_in,
    words_out,
    g_alt,
    g_out,
    g_in,
    load_sem,
    t_send,
    t_recv,
    w_send,
    w_recv,
    g_send,
    g_recv,
    go,
    anchor_ref,
    live_ref,
):
    n_depth, n_sx, n_sy = sizes
    d, sx, sy = lax.axis_index("depth"), lax.axis_index("sx"), lax.axis_index("sy")
    last = n_depth - 1

    def at(dx, dy):
        return (d, lax.rem(sx + dx + n_sx, n_sx), lax.rem(sy + dy + n_sy, n_sy))

    around = [(i, j) for i in (-1, 0, 1) for j in (-1, 0, 1) if (i, j) != (0, 0)]

    barrier = pltpu.get_barrier_semaphore()
    for i, j in around:
        pl.semaphore_signal(barrier, inc=1, device_id=at(i, j), device_id_type=MESH)


    @pl.when(d > 0)
    def _():
        pl.semaphore_signal(barrier, inc=1, device_id=(d - 1, sx, sy), device_id_type=MESH)

    @pl.when(d < last)
    def _():
        pl.semaphore_signal(barrier, inc=1, device_id=(d + 1, sx, sy), device_id_type=MESH)

    loads = [
        pltpu.make_async_copy(src, dst, load_sem.at[i])
        for i, (src, dst) in enumerate(
            [
                (phase_hbm, phase),
                (m_hbm, m_v),
                (rows_hbm, rows_v),
                (exit_hbm, exit_v),
                (inc_hbm, inc),
                (t_hbm, t_own),
                (anchor_hbm, anchor_ref),
                (live_hbm, live_ref),
            ]
        )
    ]
    for c in loads:
        c.start()

    ends = jnp.where(d > 0, 1, 0) + jnp.where(d < last, 1, 0)
    pl.semaphore_wait(barrier, len(around) + ends)

    full = pl.ds(0, TILE)
    part = [pl.ds(0, HALF), pl.ds(HALF, HALF)]
    toward = [-1, 1]
    pieces = (
        [(0, part[p], full, (toward[p], 0)) for p in (0, 1)]
        + [(1, full, part[q], (0, toward[q])) for q in (0, 1)]
        + [(2, part[p], part[q], (toward[p], toward[q])) for p in (0, 1) for q in (0, 1)]
    )

    both = pl.ds(0, 2)
    one = [pl.ds(0, 1), pl.ds(1, 1)]
    blocks = (
        [(0, (one[p], both), (toward[p], 0)) for p in (0, 1)]
        + [(1, (both, one[q]), (0, toward[q])) for q in (0, 1)]
        + [(2, (one[p], one[q]), (toward[p], toward[q])) for p in (0, 1) for q in (0, 1)]
    )

    def t_copies(li):
        return [
            pltpu.make_async_remote_copy(
                src_ref=t_hbm.at[li, :, rows, lanes],
                dst_ref=t_alt.at[li, kind, :, rows, lanes],
                send_sem=t_send.at[li * 8 + i],
                recv_sem=t_recv.at[li * 8 + i],
                device_id=at(*way),
                device_id_type=MESH,
            )
            for i, (kind, rows, lanes, way) in enumerate(pieces)
        ]

    def g_copies(li):
        return [
            pltpu.make_async_remote_copy(
                src_ref=g_out.at[li, kind, block[0], block[1]],
                dst_ref=g_in.at[li, kind, block[0], block[1]],
                send_sem=g_send.at[li * 8 + i],
                recv_sem=g_recv.at[li * 8 + i],
                device_id=at(-way[0], -way[1]),
                device_id_type=MESH,
            )
            for i, (kind, block, way) in enumerate(blocks)
        ]

    def w_copy(slot, h):
        return pltpu.make_async_remote_copy(
            src_ref=words_out.at[slot, h],
            dst_ref=words_in.at[slot, h],
            send_sem=w_send.at[slot * 2 + h],
            recv_sem=w_recv.at[slot * 2 + h],
            device_id=(lax.rem(d + last, n_depth), sx, sy),
            device_id_type=MESH,
        )

    odd = lax.rem(d, 2) == 1

    def share():
        for li in (1, 0):
            for c in reversed(t_copies(li)):
                c.start()

    @pl.when(odd)
    def _():
        share()

    def offsets(slot):
        return anchor_ref[slot, 0] - sx * TILE, anchor_ref[slot, 1] - sy * TILE

    quads = [(0, 0), (0, 1), (1, 0), (1, 1)]

    def masks(slot, p, q):
        out = []
        for a, half, dim in zip(offsets(slot), (p, q), (0, 1)):
            k = lax.broadcasted_iota(jnp.int32, (HALF, HALF), dim)
            out.append(k >= a if half == 0 else k < a + HALF)
        return out

    def rolled(slot, fields):
        ax, ay = offsets(slot)
        i = lax.broadcasted_iota(jnp.int32, (TILE, TILE), 0)
        j = lax.broadcasted_iota(jnp.int32, (TILE, TILE), 1)
        by_rows = jnp.where(((j + ax - i) & (TILE - 1)) == 0, 1.0, 0.0).astype(BF16)
        by_lanes = jnp.where(((i + ay - j) & (TILE - 1)) == 0, 1.0, 0.0).astype(BF16)
        return [dot(by_rows, dot(f, by_lanes).astype(BF16)) for f in fields]

    for c in loads:
        c.wait()

    @pl.when(d == last)
    def _():
        for slot in (0, 1):
            alive = jnp.where(slot < live_ref[0], 1.0, 0.0).astype(F32)
            for k, f in enumerate(rolled(slot, [exit_v[slot, 0], exit_v[slot, 1]])):
                for h in (0, 1):
                    waves[slot, h, k] = f[h * HALF : (h + 1) * HALF] * alive

    i = lax.broadcasted_iota(jnp.int32, (TILE, TILE), 0)
    j = lax.broadcasted_iota(jnp.int32, (TILE, TILE), 1)
    deal = jnp.where(i == jnp.where(j < HALF, 2 * j, 2 * j - (TILE - 1)), 1.0, 0.0).astype(BF16)
    deal_rows = jnp.where(j == jnp.where(i < HALF, 2 * i, 2 * i - (TILE - 1)), 1.0, 0.0).astype(BF16)
    p = phase[...]
    p0 = p.astype(BF16)
    p1, p2 = halves(p - p0.astype(F32))
    f0, f1, f2 = [dot(deal_rows, dot(q, deal).astype(BF16)) for q in (p0, p1, p2)]
    phase[...] = (f0 + f1) + f2
    for h in (0, 1):
        ordered = phase[part[h], :]
        for k, f in enumerate((jnp.cos(ordered), jnp.sin(ordered))):
            for g in (0, 1):
                rot[k, g, :, part[h]] = f[:, g * HALF : (g + 1) * HALF]

    def roll_incident(slot):
        got = rolled(slot, [inc[li, slot, k] for li in (0, 1) for k in (0, 1)])
        for n, f in enumerate(got):
            inc[n // 2, slot, n % 2] = f.astype(BF16)

    for slot in (0, 1):
        roll_incident(slot)

    zero = jnp.zeros((HALF, HALF), F32)

    def window(li, slot):
        for p, q in quads:
            on_x, on_y = masks(slot, p, q)
            spot = (part[p], part[q])
            for k in (0, 1):
                here = t_own[(li, k) + spot].astype(F32)
                tx, ty, txy = [t_alt[(li, kind, k) + spot].astype(F32) for kind in range(3)]
                t_eff[(li, slot, k) + spot] = jnp.where(
                    on_x, jnp.where(on_y, here, ty), jnp.where(on_y, tx, txy)
                ).astype(BF16)

    first_chip = d >= last - 1

    def border(li):
        for p in (0, 1):
            edge_x, edge_y = [(n - 1, 0)[p] for n in (n_sx, n_sy)]

            @pl.when(sx == edge_x)
            def _(p=p):
                for kind in (0, 2):
                    t_alt[li, kind, :, part[p], :] = jnp.zeros((2, HALF, TILE), BF16)

            @pl.when(sy == edge_y)
            def _(p=p):
                for kind in (1, 2):
                    t_alt[li, kind, :, :, part[p]] = jnp.zeros((2, TILE, HALF), BF16)

    def windows(li):
        for c in t_copies(li)[1 if li == 1 else 0 :]:
            c.wait_recv()
        border(li)
        window(li, 0)

        @pl.when(jnp.logical_not(first_chip))
        def _():
            window(li, 1)

    def beside(a, b):
        return jnp.concatenate([a, b], axis=1)

    def above(a, b):
        return jnp.concatenate([a, b], axis=0)

    def right(z, first):
        head, tail = halves(z)
        table = jnp.concatenate([m_v[first], m_v[first], m_v[first + 1]], axis=0)
        rows = jnp.concatenate([head, tail, head], axis=1)
        parts = []
        for r in (slice(0, HALF), slice(HALF, 2 * HALF)):
            two = dot(above(head[r], tail[r]), m_v[first])
            parts.append((two[:HALF] + two[HALF:]) + dot(head[r], m_v[first + 1]))
        return above(*parts)

    def left(z, first):
        head, tail = halves(z)
        table = jnp.concatenate([m_v[first], m_v[first + 1], m_v[first]], axis=1)
        cols = jnp.concatenate([head, head, tail], axis=0)
        parts = []
        for r in (slice(0, HALF), slice(HALF, 2 * HALF)):
            two = dot(above(m_v[first, r], m_v[first + 1, r]), head)
            parts.append((two[:HALF] + two[HALF:]) + dot(m_v[first, r], tail))
        return above(*parts)

    c, s = rows_v[0], rows_v[1]

    def between(y):
        a, b = y[:HALF], y[HALF:]
        sm, df = a + b, a - b
        dr, di = df[:, :HALF], df[:, HALF:]
        return above(beside(sm[:, :HALF], dr * c + di * s), beside(sm[:, HALF:], di * c - dr * s))

    def turned(g, x):
        xr, xi = x[:HALF], x[HALF:]
        cp, sp = rot[0, g], rot[1, g]
        return above(xr * cp + xi * sp, xi * cp - xr * sp)

    def undealt(e):
        er, ei = e[:HALF, HALF:], e[HALF:, HALF:]
        tr, ti = er * c - ei * s, ei * c + er * s
        vr, vi = e[:HALF, :HALF], e[HALF:, :HALF]
        return above(beside(vr + tr, vi + ti), beside(vr - tr, vi - ti))

    def finish(joined, store):
        for h in (0, 1):
            e, o = [j[h * HALF : (h + 1) * HALF] for j in joined]
            low, high = e + o, e - o
            store(h, low[:, :HALF], high[:, :HALF], low[:, HALF:], high[:, HALF:])

    def propagated(fields):
        a = [beside(re[:, :HALF], im[:, :HALF]) for re, im in fields]
        b = [beside(re[:, HALF:], im[:, HALF:]) for re, im in fields]
        z0 = above(a[0] + b[0], a[1] + b[1])
        z1 = above(a[0] - b[0], a[1] - b[1])

        y0 = right(z0, 2)
        y1 = right(z1, 6)
        x0 = left(between(y0), 0)
        x1 = left(between(y1), 0)
        e0 = left(turned(0, x0), 2)
        e1 = left(turned(1, x1), 2)
        return [right(undealt(e0), 0), right(undealt(e1), 4)]

    def through(li, slot, h, re, im):
        rows = part[h]
        tr = t_eff[li, slot, 0, rows, :].astype(F32)
        ti = t_eff[li, slot, 1, rows, :].astype(F32)
        return conj_times(tr, ti, re, im)

    def shares(li, slot, p, q):
        wave = waves if li == 1 else middle
        er = inc[li, slot, 0, part[p], part[q]].astype(F32)
        ei = inc[li, slot, 1, part[p], part[q]].astype(F32)
        on_x, on_y = masks(slot, p, q)
        out = []
        for t in conj_times(er, ei, wave[slot, p, 0, :, part[q]], wave[slot, p, 1, :, part[q]]):
            inside = jnp.where(on_x, t, zero)
            beyond = jnp.where(on_x, zero, t)
            out.append(
                [
                    jnp.where(on_y, inside, zero),
                    jnp.where(on_y, beyond, zero),
                    jnp.where(on_y, zero, inside),
                    jnp.where(on_y, zero, beyond),
                ]
            )
        return out

    def first_gradient(li):
        for p, q in quads:
            spot = (part[p], part[q])
            for k, t in enumerate(shares(li, 0, p, q)):
                own[(li, k) + spot] = t[0]
                for kind in range(3):
                    g_alt[(li, kind, k) + spot] = t[kind + 1]

    def second_gradient(li):
        copies = g_copies(li)
        for p, q in quads:
            spot = (part[p], part[q])
            re, im = shares(li, 1, p, q)
            for kind in (2, 0, 1):
                g_out[li, kind, p, q] = coded(
                    g_alt[(li, kind, 0) + spot] + re[kind + 1], g_alt[(li, kind, 1) + spot] + im[kind + 1]
                )
            copies[4 + 2 * p + q].start()
            if q == 1:
                copies[p].start()
            if p == 1:
                copies[2 + q].start()
            own[(li, 0) + spot] += re[0]
            own[(li, 1) + spot] += im[0]

    def gradient(li, slot):
        @pl.when(slot == 0)
        def _():
            first_gradient(li)

        @pl.when(slot == 1)
        def _():
            second_gradient(li)

    def apply_layer(li, slot, source, store):
        fields = [through(li, slot, h, source[slot, h, 0], source[slot, h, 1]) for h in (0, 1)]
        finish(propagated(fields), store)

    @pl.when(odd)
    def _():
        t_copies(1)[0].wait_recv()
        pl.semaphore_signal(go, inc=1, device_id=(d - 1, sx, sy), device_id_type=MESH)

    @pl.when(jnp.logical_not(odd))
    def _():
        pl.semaphore_wait(go, 1)
        share()
        t_copies(1)[0].wait_recv()

    windows(1)

    early = d < 2

    def one_slot(slot, carry):
        @pl.when(d < last)
        def _():
            for h in (0, 1):
                w_copy(slot, h).wait_recv()
                for q in (0, 1):
                    re, im = decoded(words_in[slot, h, q])
                    waves[slot, h, 0, :, part[q]] = re
                    waves[slot, h, 1, :, part[q]] = im

        @pl.when(early)
        def _():
            gradient(1, slot)

        def keep(h, lr, hr, li_, hi_):
            middle[slot, h, 0, :, :HALF] = lr
            middle[slot, h, 0, :, HALF:] = hr
            middle[slot, h, 1, :, :HALF] = li_
            middle[slot, h, 1, :, HALF:] = hi_

        apply_layer(1, slot, waves, keep)

        @pl.when(slot == 0)
        def _():
            windows(0)

        @pl.when(early)
        def _():
            gradient(0, slot)

        @pl.when(d > 0)
        def _():
            def encode(h, lr, hr, li_, hi_):
                words_out[slot, h, 0] = coded(lr, li_)
                words_out[slot, h, 1] = coded(hr, hi_)
                w_copy(slot, h).start()

            apply_layer(0, slot, middle, encode)

        @pl.when(jnp.logical_and(first_chip, slot == 0))
        def _():
            for li in (1, 0):
                window(li, 1)

        return carry

    lax.fori_loop(0, 2, one_slot, 0)

    @pl.when(jnp.logical_not(early))
    def _():
        for li in (1, 0):
            first_gradient(li)
            second_gradient(li)

    for li in (1, 0):
        for c in t_copies(li):
            c.wait_send()

    @pl.when(d > 0)
    def _():
        for slot in (0, 1):
            for h in (0, 1):
                w_copy(slot, h).wait_send()

    from_x = [jnp.where(sx > 0, 1.0, 0.0), jnp.where(sx < n_sx - 1, 1.0, 0.0)]
    from_y = [jnp.where(sy > 0, 1.0, 0.0), jnp.where(sy < n_sy - 1, 1.0, 0.0)]
    for li in (1, 0):
        copies = g_copies(li)
        for p, q in quads:
            if q == 0:
                copies[p].wait_recv()
            if p == 0:
                copies[2 + q].wait_recv()
            copies[4 + 2 * p + q].wait_recv()
            weights = (from_x[p], from_y[q], from_x[p] * from_y[q])
            got = [decoded(g_in[li, kind, p, q], weights[kind] / 32767.0) for kind in range(3)]
            for k in (0, 1):
                own[li, k, part[p], part[q]] += (got[0][k] + got[1][k]) + got[2][k]

    for li in (1, 0):
        for c in g_copies(li):
            c.wait_send()


def shards(transmission, incident, exit_adjoint, propagator_phase, scan_anchor, live_count):
    sizes = tuple(lax.axis_size(a) for a in ("depth", "sx", "sy"))
    slab = transmission.shape[0]
    any_space = pl.BlockSpec(memory_space=pl.ANY)
    plane = (TILE, TILE)
    dma = pltpu.SemaphoreType.DMA
    return pl.pallas_call(
        functools.partial(kernel, sizes),
        out_shape=pltpu.VMEM(transmission.shape, F32),
        in_specs=[any_space] * 8,
        out_specs=pl.BlockSpec(memory_space=pltpu.VMEM),
        scratch_shapes=[
            pltpu.VMEM((slab, 2) + plane, BF16),
            pltpu.VMEM((slab, 3, 2) + plane, BF16),
            pltpu.VMEM((slab, 2, 2) + plane, BF16),
            pltpu.VMEM((slab, 2, 2) + plane, BF16),
            pltpu.VMEM((2, 2) + plane, BF16),
            pltpu.VMEM(plane, F32),
            pltpu.VMEM((2, 2, HALF, TILE), F32),
            pltpu.VMEM((8,) + plane, BF16),
            pltpu.VMEM((2, HALF, HALF), F32),
            pltpu.VMEM((2, 2, 2, HALF, TILE), F32),
            pltpu.VMEM((2, 2, 2, HALF, TILE), F32),
            pltpu.VMEM((2, 2, 2, CODED, HALF), jnp.int32),
            pltpu.VMEM((2, 2, 2, CODED, HALF), jnp.int32),
            pltpu.VMEM((slab, 3, 2) + plane, F32),
            pltpu.VMEM((slab, 3, 2, 2, CODED, HALF), jnp.int32),
            pltpu.VMEM((slab, 3, 2, 2, CODED, HALF), jnp.int32),
            dma((8,)),
            dma((16,)),
            dma((16,)),
            dma((4,)),
            dma((4,)),
            dma((16,)),
            dma((16,)),
            pltpu.SemaphoreType.REGULAR,
            pltpu.SMEM((2, 2), jnp.int32),
            pltpu.SMEM((1,), jnp.int32),
        ],
        compiler_params=pltpu.CompilerParams(
            collective_id=0, has_side_effects=True, vmem_limit_bytes=60 * 1024 * 1024
        ),
    )(
        transmission,
        incident,
        exit_adjoint,
        propagator_phase,
        jnp.asarray(dft_tables()),
        jnp.asarray(row_twiddles()),
        scan_anchor,
        live_count,
    )


def solution(mesh):
    placed = (
        P("depth", None, "sx", "sy"),
        P("depth", ("sx", "sy"), None, None, None),
        P(("sx", "sy"), None, None, None),
        P(),
        P(("sx", "sy"), None),
        P(("sx", "sy")),
    )
    return jax.shard_map(
        shards, mesh=mesh, in_specs=placed, out_specs=P("depth", None, "sx", "sy"), check_vma=False
    )
```

```python
import functools

import ml_dtypes
import numpy as np
import jax
import jax.numpy as jnp
from jax import lax
from jax.experimental import pallas as pl
from jax.experimental.pallas import tpu as pltpu
from jax.sharding import PartitionSpec as P

TILE = 256
HALF = 128
GROUPS = HALF // 8
CODED = HALF + 8
MESH = pl.DeviceIdType.MESH
F32 = jnp.float32
BF16 = jnp.bfloat16


def dft_tables():
    n = np.arange(HALF)
    out = []
    for odd in (0, 1):
        angle = 2.0 * np.pi * (((2 * n[:, None] + odd) * n[None, :]) % TILE) / TILE
        c, s = np.cos(angle) / 16.0, np.sin(angle) / 16.0
        m = np.block([[c, s], [-s, c]])
        for a in (m, m.T):
            head = a.astype(ml_dtypes.bfloat16)
            out += [head, (a - head.astype(np.float64)).astype(ml_dtypes.bfloat16)]
    return np.stack(out)


def row_twiddles():
    n = 2.0 * np.pi * np.arange(HALF) / TILE
    both = np.stack([np.cos(n), np.sin(n)])
    return np.broadcast_to(both[:, :, None], (2, HALF, HALF)).astype(np.float32)


def halves(x):
    head = x.astype(BF16)
    return head, (x - head.astype(F32)).astype(BF16)


def conj_times(ar, ai, br, bi):
    return ar * br + ai * bi, ar * bi - ai * br


def spread(x):
    return jnp.concatenate([x] * GROUPS, axis=0)


def coded(re, im):
    top = jnp.maximum(jnp.abs(re), jnp.abs(im))
    parts = [top[8 * g : 8 * g + 8] for g in range(GROUPS)]
    while len(parts) > 1:
        parts = [jnp.maximum(a, b) for a, b in zip(parts[::2], parts[1::2])]
    steps = (jnp.log2(jnp.maximum(parts[0], 1e-33)) * 8.0).astype(jnp.int32) + 2
    unit = spread(32767.0 / jnp.exp2(steps.astype(F32) * 0.125))
    high = (re * unit + 32768.5).astype(jnp.int32)
    low = (im * unit + 32768.5).astype(jnp.int32)
    return jnp.concatenate([(high << 16) | low, steps], axis=0)


def decoded(words, weight=1.0 / 32767.0):
    unit = spread(jnp.exp2(words[HALF:].astype(F32) * 0.125) * weight)
    body = words[:HALF]
    high = ((body >> 16) & 65535).astype(F32) - 32768.0
    low = (body & 65535).astype(F32) - 32768.0
    return high * unit, low * unit


def dot(a, b):
    return jnp.dot(a, b, preferred_element_type=F32)


def kernel(
    sizes,
    t_hbm,
    inc_hbm,
    exit_hbm,
    phase_hbm,
    m_hbm,
    rows_hbm,
    anchor_hbm,
    live_hbm,
    own,
    t_own,
    t_alt,
    t_eff,
    inc,
    exit_v,
    phase,
    rot,
    m_v,
    rows_v,
    waves,
    middle,
    words_in,
    words_out,
    g_alt,
    g_out,
    g_in,
    load_sem,
    t_send,
    t_recv,
    w_send,
    w_recv,
    g_send,
    g_recv,
    go,
    anchor_ref,
    live_ref,
):
    n_depth, n_sx, n_sy = sizes
    d, sx, sy = lax.axis_index("depth"), lax.axis_index("sx"), lax.axis_index("sy")
    last = n_depth - 1

    def at(dx, dy):
        return (d, lax.rem(sx + dx + n_sx, n_sx), lax.rem(sy + dy + n_sy, n_sy))

    around = [(i, j) for i in (-1, 0, 1) for j in (-1, 0, 1) if (i, j) != (0, 0)]

    barrier = pltpu.get_barrier_semaphore()
    for i, j in around:
        pl.semaphore_signal(barrier, inc=1, device_id=at(i, j), device_id_type=MESH)


    @pl.when(d > 0)
    def _():
        pl.semaphore_signal(barrier, inc=1, device_id=(d - 1, sx, sy), device_id_type=MESH)

    @pl.when(d < last)
    def _():
        pl.semaphore_signal(barrier, inc=1, device_id=(d + 1, sx, sy), device_id_type=MESH)

    loads = [
        pltpu.make_async_copy(src, dst, load_sem.at[i])
        for i, (src, dst) in enumerate(
            [
                (phase_hbm, phase),
                (m_hbm, m_v),
                (rows_hbm, rows_v),
                (exit_hbm, exit_v),
                (inc_hbm, inc),
                (t_hbm, t_own),
                (anchor_hbm, anchor_ref),
                (live_hbm, live_ref),
            ]
        )
    ]
    for c in loads:
        c.start()

    ends = jnp.where(d > 0, 1, 0) + jnp.where(d < last, 1, 0)
    pl.semaphore_wait(barrier, len(around) + ends)

    full = pl.ds(0, TILE)
    part = [pl.ds(0, HALF), pl.ds(HALF, HALF)]
    toward = [-1, 1]
    pieces = (
        [(0, part[p], full, (toward[p], 0)) for p in (0, 1)]
        + [(1, full, part[q], (0, toward[q])) for q in (0, 1)]
        + [(2, part[p], part[q], (toward[p], toward[q])) for p in (0, 1) for q in (0, 1)]
    )

    both = pl.ds(0, 2)
    one = [pl.ds(0, 1), pl.ds(1, 1)]
    blocks = (
        [(0, (one[p], both), (toward[p], 0)) for p in (0, 1)]
        + [(1, (both, one[q]), (0, toward[q])) for q in (0, 1)]
        + [(2, (one[p], one[q]), (toward[p], toward[q])) for p in (0, 1) for q in (0, 1)]
    )

    def t_copies(li):
        return [
            pltpu.make_async_remote_copy(
                src_ref=t_hbm.at[li, :, rows, lanes],
                dst_ref=t_alt.at[li, kind, :, rows, lanes],
                send_sem=t_send.at[li * 8 + i],
                recv_sem=t_recv.at[li * 8 + i],
                device_id=at(*way),
                device_id_type=MESH,
            )
            for i, (kind, rows, lanes, way) in enumerate(pieces)
        ]

    def g_copies(li):
        return [
            pltpu.make_async_remote_copy(
                src_ref=g_out.at[li, kind, block[0], block[1]],
                dst_ref=g_in.at[li, kind, block[0], block[1]],
                send_sem=g_send.at[li * 8 + i],
                recv_sem=g_recv.at[li * 8 + i],
                device_id=at(-way[0], -way[1]),
                device_id_type=MESH,
            )
            for i, (kind, block, way) in enumerate(blocks)
        ]

    def w_copy(slot, h):
        return pltpu.make_async_remote_copy(
            src_ref=words_out.at[slot, h],
            dst_ref=words_in.at[slot, h],
            send_sem=w_send.at[slot * 2 + h],
            recv_sem=w_recv.at[slot * 2 + h],
            device_id=(lax.rem(d + last, n_depth), sx, sy),
            device_id_type=MESH,
        )

    odd = lax.rem(d, 2) == 1

    def share():
        for li in (1, 0):
            for c in reversed(t_copies(li)):
                c.start()

    @pl.when(odd)
    def _():
        share()

    def offsets(slot):
        return anchor_ref[slot, 0] - sx * TILE, anchor_ref[slot, 1] - sy * TILE

    quads = [(0, 0), (0, 1), (1, 0), (1, 1)]

    def masks(slot, p, q):
        out = []
        for a, half, dim in zip(offsets(slot), (p, q), (0, 1)):
            k = lax.broadcasted_iota(jnp.int32, (HALF, HALF), dim)
            out.append(k >= a if half == 0 else k < a + HALF)
        return out

    def rolled(slot, fields):
        ax, ay = offsets(slot)
        i = lax.broadcasted_iota(jnp.int32, (TILE, TILE), 0)
        j = lax.broadcasted_iota(jnp.int32, (TILE, TILE), 1)
        by_rows = jnp.where(((j + ax - i) & (TILE - 1)) == 0, 1.0, 0.0).astype(BF16)
        by_lanes = jnp.where(((i + ay - j) & (TILE - 1)) == 0, 1.0, 0.0).astype(BF16)
        return [dot(by_rows, dot(f, by_lanes).astype(BF16)) for f in fields]

    for c in loads:
        c.wait()

    @pl.when(d == last)
    def _():
        for slot in (0, 1):
            alive = jnp.where(slot < live_ref[0], 1.0, 0.0).astype(F32)
            for k, f in enumerate(rolled(slot, [exit_v[slot, 0], exit_v[slot, 1]])):
                for h in (0, 1):
                    waves[slot, h, k] = f[h * HALF : (h + 1) * HALF] * alive

    i = lax.broadcasted_iota(jnp.int32, (TILE, TILE), 0)
    j = lax.broadcasted_iota(jnp.int32, (TILE, TILE), 1)
    deal = jnp.where(i == jnp.where(j < HALF, 2 * j, 2 * j - (TILE - 1)), 1.0, 0.0).astype(BF16)
    deal_rows = jnp.where(j == jnp.where(i < HALF, 2 * i, 2 * i - (TILE - 1)), 1.0, 0.0).astype(BF16)
    p = phase[...]
    p0 = p.astype(BF16)
    p1, p2 = halves(p - p0.astype(F32))
    f0, f1, f2 = [dot(deal_rows, dot(q, deal).astype(BF16)) for q in (p0, p1, p2)]
    phase[...] = (f0 + f1) + f2
    for h in (0, 1):
        ordered = phase[part[h], :]
        for k, f in enumerate((jnp.cos(ordered), jnp.sin(ordered))):
            for g in (0, 1):
                rot[k, g, :, part[h]] = f[:, g * HALF : (g + 1) * HALF]

    def roll_incident(slot):
        got = rolled(slot, [inc[li, slot, k] for li in (0, 1) for k in (0, 1)])
        for n, f in enumerate(got):
            inc[n // 2, slot, n % 2] = f.astype(BF16)

    for slot in (0, 1):
        roll_incident(slot)

    zero = jnp.zeros((HALF, HALF), F32)

    def window(li, slot):
        for p, q in quads:
            on_x, on_y = masks(slot, p, q)
            spot = (part[p], part[q])
            for k in (0, 1):
                here = t_own[(li, k) + spot].astype(F32)
                tx, ty, txy = [t_alt[(li, kind, k) + spot].astype(F32) for kind in range(3)]
                t_eff[(li, slot, k) + spot] = jnp.where(
                    on_x, jnp.where(on_y, here, ty), jnp.where(on_y, tx, txy)
                ).astype(BF16)

    def border(li):
        for p in (0, 1):
            edge_x, edge_y = [(n - 1, 0)[p] for n in (n_sx, n_sy)]

            @pl.when(sx == edge_x)
            def _(p=p):
                for kind in (0, 2):
                    t_alt[li, kind, :, part[p], :] = jnp.zeros((2, HALF, TILE), BF16)

            @pl.when(sy == edge_y)
            def _(p=p):
                for kind in (1, 2):
                    t_alt[li, kind, :, :, part[p]] = jnp.zeros((2, TILE, HALF), BF16)

    def windows(li):
        for c in t_copies(li)[1 if li == 1 else 0 :]:
            c.wait_recv()
        border(li)
        for slot in (0, 1):
            window(li, slot)

    def beside(a, b):
        return jnp.concatenate([a, b], axis=1)

    def above(a, b):
        return jnp.concatenate([a, b], axis=0)

    def right(z, first):
        head, tail = halves(z)
        table = jnp.concatenate([m_v[first], m_v[first], m_v[first + 1]], axis=0)
        rows = jnp.concatenate([head, tail, head], axis=1)
        parts = []
        for r in (slice(0, HALF), slice(HALF, 2 * HALF)):
            two = dot(above(head[r], tail[r]), m_v[first])
            parts.append((two[:HALF] + two[HALF:]) + dot(head[r], m_v[first + 1]))
        return above(*parts)

    def left(z, first):
        head, tail = halves(z)
        table = jnp.concatenate([m_v[first], m_v[first + 1], m_v[first]], axis=1)
        cols = jnp.concatenate([head, head, tail], axis=0)
        parts = []
        for r in (slice(0, HALF), slice(HALF, 2 * HALF)):
            two = dot(above(m_v[first, r], m_v[first + 1, r]), head)
            parts.append((two[:HALF] + two[HALF:]) + dot(m_v[first, r], tail))
        return above(*parts)

    c, s = rows_v[0], rows_v[1]

    def between(y):
        a, b = y[:HALF], y[HALF:]
        sm, df = a + b, a - b
        dr, di = df[:, :HALF], df[:, HALF:]
        return above(beside(sm[:, :HALF], dr * c + di * s), beside(sm[:, HALF:], di * c - dr * s))

    def turned(g, x):
        xr, xi = x[:HALF], x[HALF:]
        cp, sp = rot[0, g], rot[1, g]
        return above(xr * cp + xi * sp, xi * cp - xr * sp)

    def undealt(e):
        er, ei = e[:HALF, HALF:], e[HALF:, HALF:]
        tr, ti = er * c - ei * s, ei * c + er * s
        vr, vi = e[:HALF, :HALF], e[HALF:, :HALF]
        return above(beside(vr + tr, vi + ti), beside(vr - tr, vi - ti))

    def finish(joined, store):
        for h in (0, 1):
            e, o = [j[h * HALF : (h + 1) * HALF] for j in joined]
            low, high = e + o, e - o
            store(h, low[:, :HALF], high[:, :HALF], low[:, HALF:], high[:, HALF:])

    def propagated(fields):
        a = [beside(re[:, :HALF], im[:, :HALF]) for re, im in fields]
        b = [beside(re[:, HALF:], im[:, HALF:]) for re, im in fields]
        z0 = above(a[0] + b[0], a[1] + b[1])
        z1 = above(a[0] - b[0], a[1] - b[1])

        y0 = right(z0, 2)
        y1 = right(z1, 6)
        x0 = left(between(y0), 0)
        x1 = left(between(y1), 0)
        e0 = left(turned(0, x0), 2)
        e1 = left(turned(1, x1), 2)
        return [right(undealt(e0), 0), right(undealt(e1), 4)]

    def through(li, slot, h, re, im):
        rows = part[h]
        tr = t_eff[li, slot, 0, rows, :].astype(F32)
        ti = t_eff[li, slot, 1, rows, :].astype(F32)
        return conj_times(tr, ti, re, im)

    def shares(li, slot, p, q):
        wave = waves if li == 1 else middle
        er = inc[li, slot, 0, part[p], part[q]].astype(F32)
        ei = inc[li, slot, 1, part[p], part[q]].astype(F32)
        on_x, on_y = masks(slot, p, q)
        out = []
        for t in conj_times(er, ei, wave[slot, p, 0, :, part[q]], wave[slot, p, 1, :, part[q]]):
            inside = jnp.where(on_x, t, zero)
            beyond = jnp.where(on_x, zero, t)
            out.append(
                [
                    jnp.where(on_y, inside, zero),
                    jnp.where(on_y, beyond, zero),
                    jnp.where(on_y, zero, inside),
                    jnp.where(on_y, zero, beyond),
                ]
            )
        return out

    def first_gradient(li):
        for p, q in quads:
            spot = (part[p], part[q])
            for k, t in enumerate(shares(li, 0, p, q)):
                own[(li, k) + spot] = t[0]
                for kind in range(3):
                    g_alt[(li, kind, k) + spot] = t[kind + 1]

    def second_gradient(li):
        copies = g_copies(li)
        for p, q in quads:
            spot = (part[p], part[q])
            re, im = shares(li, 1, p, q)
            for kind in (2, 0, 1):
                g_out[li, kind, p, q] = coded(
                    g_alt[(li, kind, 0) + spot] + re[kind + 1], g_alt[(li, kind, 1) + spot] + im[kind + 1]
                )
            copies[4 + 2 * p + q].start()
            if q == 1:
                copies[p].start()
            if p == 1:
                copies[2 + q].start()
            own[(li, 0) + spot] += re[0]
            own[(li, 1) + spot] += im[0]

    def gradient(li, slot):
        @pl.when(slot == 0)
        def _():
            first_gradient(li)

        @pl.when(slot == 1)
        def _():
            second_gradient(li)

    def apply_layer(li, slot, source, store):
        fields = [through(li, slot, h, source[slot, h, 0], source[slot, h, 1]) for h in (0, 1)]
        finish(propagated(fields), store)

    @pl.when(odd)
    def _():
        t_copies(1)[0].wait_recv()
        pl.semaphore_signal(go, inc=1, device_id=(d - 1, sx, sy), device_id_type=MESH)

    @pl.when(jnp.logical_not(odd))
    def _():
        pl.semaphore_wait(go, 1)
        share()
        t_copies(1)[0].wait_recv()

    windows(1)

    early = d < 2

    def one_slot(slot, carry):
        @pl.when(d < last)
        def _():
            for h in (0, 1):
                w_copy(slot, h).wait_recv()
                for q in (0, 1):
                    re, im = decoded(words_in[slot, h, q])
                    waves[slot, h, 0, :, part[q]] = re
                    waves[slot, h, 1, :, part[q]] = im

        @pl.when(early)
        def _():
            gradient(1, slot)

        def keep(h, lr, hr, li_, hi_):
            middle[slot, h, 0, :, :HALF] = lr
            middle[slot, h, 0, :, HALF:] = hr
            middle[slot, h, 1, :, :HALF] = li_
            middle[slot, h, 1, :, HALF:] = hi_

        apply_layer(1, slot, waves, keep)

        @pl.when(slot == 0)
        def _():
            windows(0)

        @pl.when(d > 0)
        def _():
            def encode(h, lr, hr, li_, hi_):
                words_out[slot, h, 0] = coded(lr, li_)
                words_out[slot, h, 1] = coded(hr, hi_)
                w_copy(slot, h).start()

            apply_layer(0, slot, middle, encode)

        @pl.when(early)
        def _():
            gradient(0, slot)

        return carry

    lax.fori_loop(0, 2, one_slot, 0)

    @pl.when(jnp.logical_not(early))
    def _():
        for li in (1, 0):
            first_gradient(li)
            second_gradient(li)

    for li in (1, 0):
        for c in t_copies(li):
            c.wait_send()

    @pl.when(d > 0)
    def _():
        for slot in (0, 1):
            for h in (0, 1):
                w_copy(slot, h).wait_send()

    from_x = [jnp.where(sx > 0, 1.0, 0.0), jnp.where(sx < n_sx - 1, 1.0, 0.0)]
    from_y = [jnp.where(sy > 0, 1.0, 0.0), jnp.where(sy < n_sy - 1, 1.0, 0.0)]
    for li in (1, 0):
        copies = g_copies(li)
        for p, q in quads:
            if q == 0:
                copies[p].wait_recv()
            if p == 0:
                copies[2 + q].wait_recv()
            copies[4 + 2 * p + q].wait_recv()
            weights = (from_x[p], from_y[q], from_x[p] * from_y[q])
            got = [decoded(g_in[li, kind, p, q], weights[kind] / 32767.0) for kind in range(3)]
            for k in (0, 1):
                own[li, k, part[p], part[q]] += (got[0][k] + got[1][k]) + got[2][k]

    for li in (1, 0):
        for c in g_copies(li):
            c.wait_send()


def shards(transmission, incident, exit_adjoint, propagator_phase, scan_anchor, live_count):
    sizes = tuple(lax.axis_size(a) for a in ("depth", "sx", "sy"))
    slab = transmission.shape[0]
    any_space = pl.BlockSpec(memory_space=pl.ANY)
    plane = (TILE, TILE)
    dma = pltpu.SemaphoreType.DMA
    return pl.pallas_call(
        functools.partial(kernel, sizes),
        out_shape=pltpu.VMEM(transmission.shape, F32),
        in_specs=[any_space] * 8,
        out_specs=pl.BlockSpec(memory_space=pltpu.VMEM),
        scratch_shapes=[
            pltpu.VMEM((slab, 2) + plane, BF16),
            pltpu.VMEM((slab, 3, 2) + plane, BF16),
            pltpu.VMEM((slab, 2, 2) + plane, BF16),
            pltpu.VMEM((slab, 2, 2) + plane, BF16),
            pltpu.VMEM((2, 2) + plane, BF16),
            pltpu.VMEM(plane, F32),
            pltpu.VMEM((2, 2, HALF, TILE), F32),
            pltpu.VMEM((8,) + plane, BF16),
            pltpu.VMEM((2, HALF, HALF), F32),
            pltpu.VMEM((2, 2, 2, HALF, TILE), F32),
            pltpu.VMEM((2, 2, 2, HALF, TILE), F32),
            pltpu.VMEM((2, 2, 2, CODED, HALF), jnp.int32),
            pltpu.VMEM((2, 2, 2, CODED, HALF), jnp.int32),
            pltpu.VMEM((slab, 3, 2) + plane, F32),
            pltpu.VMEM((slab, 3, 2, 2, CODED, HALF), jnp.int32),
            pltpu.VMEM((slab, 3, 2, 2, CODED, HALF), jnp.int32),
            dma((8,)),
            dma((16,)),
            dma((16,)),
            dma((4,)),
            dma((4,)),
            dma((16,)),
            dma((16,)),
            pltpu.SemaphoreType.REGULAR,
            pltpu.SMEM((2, 2), jnp.int32),
            pltpu.SMEM((1,), jnp.int32),
        ],
        compiler_params=pltpu.CompilerParams(
            collective_id=0, has_side_effects=True, vmem_limit_bytes=60 * 1024 * 1024
        ),
    )(
        transmission,
        incident,
        exit_adjoint,
        propagator_phase,
        jnp.asarray(dft_tables()),
        jnp.asarray(row_twiddles()),
        scan_anchor,
        live_count,
    )


def solution(mesh):
    placed = (
        P("depth", None, "sx", "sy"),
        P("depth", ("sx", "sy"), None, None, None),
        P(("sx", "sy"), None, None, None),
        P(),
        P(("sx", "sy"), None),
        P(("sx", "sy")),
    )
    return jax.shard_map(
        shards, mesh=mesh, in_specs=placed, out_specs=P("depth", None, "sx", "sy"), check_vma=False
    )
```

```python
import functools

import ml_dtypes
import numpy as np
import jax
import jax.numpy as jnp
from jax import lax
from jax.experimental import pallas as pl
from jax.experimental.pallas import tpu as pltpu
from jax.sharding import PartitionSpec as P

TILE = 256
HALF = 128
GROUPS = HALF // 8
CODED = HALF + 8
MESH = pl.DeviceIdType.MESH
F32 = jnp.float32
BF16 = jnp.bfloat16


def dft_tables():
    n = np.arange(HALF)
    out = []
    for odd in (0, 1):
        angle = 2.0 * np.pi * (((2 * n[:, None] + odd) * n[None, :]) % TILE) / TILE
        c, s = np.cos(angle) / 16.0, np.sin(angle) / 16.0
        m = np.block([[c, s], [-s, c]])
        for a in (m, m.T):
            head = a.astype(ml_dtypes.bfloat16)
            out += [head, (a - head.astype(np.float64)).astype(ml_dtypes.bfloat16)]
    return np.stack(out)


def row_twiddles():
    n = 2.0 * np.pi * np.arange(HALF) / TILE
    both = np.stack([np.cos(n), np.sin(n)])
    return np.broadcast_to(both[:, :, None], (2, HALF, HALF)).astype(np.float32)


def halves(x):
    head = x.astype(BF16)
    return head, (x - head.astype(F32)).astype(BF16)


def conj_times(ar, ai, br, bi):
    return ar * br + ai * bi, ar * bi - ai * br


def spread(x):
    return jnp.concatenate([x] * GROUPS, axis=0)


def coded(re, im):
    top = jnp.maximum(jnp.abs(re), jnp.abs(im))
    parts = [top[8 * g : 8 * g + 8] for g in range(GROUPS)]
    while len(parts) > 1:
        parts = [jnp.maximum(a, b) for a, b in zip(parts[::2], parts[1::2])]
    steps = (jnp.log2(jnp.maximum(parts[0], 1e-33)) * 8.0).astype(jnp.int32) + 2
    unit = spread(32767.0 / jnp.exp2(steps.astype(F32) * 0.125))
    high = (re * unit + 32768.5).astype(jnp.int32)
    low = (im * unit + 32768.5).astype(jnp.int32)
    return jnp.concatenate([(high << 16) | low, steps], axis=0)


def decoded(words, weight=1.0 / 32767.0):
    unit = spread(jnp.exp2(words[HALF:].astype(F32) * 0.125) * weight)
    body = words[:HALF]
    high = ((body >> 16) & 65535).astype(F32) - 32768.0
    low = (body & 65535).astype(F32) - 32768.0
    return high * unit, low * unit


def dot(a, b):
    return jnp.dot(a, b, preferred_element_type=F32)


def kernel(
    sizes,
    t_hbm,
    inc_hbm,
    exit_hbm,
    phase_hbm,
    m_hbm,
    rows_hbm,
    anchor_hbm,
    live_hbm,
    own,
    t_own,
    t_alt,
    t_eff,
    inc,
    exit_v,
    phase,
    rot,
    m_v,
    rows_v,
    waves,
    middle,
    words_in,
    words_out,
    g_alt,
    g_out,
    g_in,
    load_sem,
    t_send,
    t_recv,
    w_send,
    w_recv,
    g_send,
    g_recv,
    go,
    anchor_ref,
    live_ref,
):
    n_depth, n_sx, n_sy = sizes
    d, sx, sy = lax.axis_index("depth"), lax.axis_index("sx"), lax.axis_index("sy")
    last = n_depth - 1

    def at(dx, dy):
        return (d, lax.rem(sx + dx + n_sx, n_sx), lax.rem(sy + dy + n_sy, n_sy))

    around = [(i, j) for i in (-1, 0, 1) for j in (-1, 0, 1) if (i, j) != (0, 0)]

    barrier = pltpu.get_barrier_semaphore()
    for i, j in around:
        pl.semaphore_signal(barrier, inc=1, device_id=at(i, j), device_id_type=MESH)


    @pl.when(d > 0)
    def _():
        pl.semaphore_signal(barrier, inc=1, device_id=(d - 1, sx, sy), device_id_type=MESH)

    @pl.when(d < last)
    def _():
        pl.semaphore_signal(barrier, inc=1, device_id=(d + 1, sx, sy), device_id_type=MESH)

    loads = [
        pltpu.make_async_copy(src, dst, load_sem.at[i])
        for i, (src, dst) in enumerate(
            [
                (phase_hbm, phase),
                (m_hbm, m_v),
                (rows_hbm, rows_v),
                (exit_hbm, exit_v),
                (inc_hbm, inc),
                (t_hbm, t_own),
                (anchor_hbm, anchor_ref),
                (live_hbm, live_ref),
            ]
        )
    ]
    for c in loads:
        c.start()

    ends = jnp.where(d > 0, 1, 0) + jnp.where(d < last, 1, 0)
    pl.semaphore_wait(barrier, len(around) + ends)

    full = pl.ds(0, TILE)
    part = [pl.ds(0, HALF), pl.ds(HALF, HALF)]
    toward = [-1, 1]
    pieces = (
        [(0, part[p], full, (toward[p], 0)) for p in (0, 1)]
        + [(1, full, part[q], (0, toward[q])) for q in (0, 1)]
        + [(2, part[p], part[q], (toward[p], toward[q])) for p in (0, 1) for q in (0, 1)]
    )

    both = pl.ds(0, 2)
    one = [pl.ds(0, 1), pl.ds(1, 1)]
    blocks = (
        [(0, (one[p], both), (toward[p], 0)) for p in (0, 1)]
        + [(1, (both, one[q]), (0, toward[q])) for q in (0, 1)]
        + [(2, (one[p], one[q]), (toward[p], toward[q])) for p in (0, 1) for q in (0, 1)]
    )

    def t_copies(li):
        return [
            pltpu.make_async_remote_copy(
                src_ref=t_hbm.at[li, :, rows, lanes],
                dst_ref=t_alt.at[li, kind, :, rows, lanes],
                send_sem=t_send.at[li * 8 + i],
                recv_sem=t_recv.at[li * 8 + i],
                device_id=at(*way),
                device_id_type=MESH,
            )
            for i, (kind, rows, lanes, way) in enumerate(pieces)
        ]

    def g_copies(li):
        return [
            pltpu.make_async_remote_copy(
                src_ref=g_out.at[li, kind, block[0], block[1]],
                dst_ref=g_in.at[li, kind, block[0], block[1]],
                send_sem=g_send.at[li * 8 + i],
                recv_sem=g_recv.at[li * 8 + i],
                device_id=at(-way[0], -way[1]),
                device_id_type=MESH,
            )
            for i, (kind, block, way) in enumerate(blocks)
        ]

    def w_copy(slot, h):
        return pltpu.make_async_remote_copy(
            src_ref=words_out.at[slot, h],
            dst_ref=words_in.at[slot, h],
            send_sem=w_send.at[slot * 2 + h],
            recv_sem=w_recv.at[slot * 2 + h],
            device_id=(lax.rem(d + last, n_depth), sx, sy),
            device_id_type=MESH,
        )

    odd = lax.rem(d, 2) == 1

    def share():
        for li in (1, 0):
            for c in reversed(t_copies(li)):
                c.start()

    @pl.when(odd)
    def _():
        share()

    def offsets(slot):
        return anchor_ref[slot, 0] - sx * TILE, anchor_ref[slot, 1] - sy * TILE

    quads = [(0, 0), (0, 1), (1, 0), (1, 1)]

    def masks(slot, p, q):
        out = []
        for a, half, dim in zip(offsets(slot), (p, q), (0, 1)):
            k = lax.broadcasted_iota(jnp.int32, (HALF, HALF), dim)
            out.append(k >= a if half == 0 else k < a + HALF)
        return out

    def rolled(slot, fields):
        ax, ay = offsets(slot)
        i = lax.broadcasted_iota(jnp.int32, (TILE, TILE), 0)
        j = lax.broadcasted_iota(jnp.int32, (TILE, TILE), 1)
        by_rows = jnp.where(((j + ax - i) & (TILE - 1)) == 0, 1.0, 0.0).astype(BF16)
        by_lanes = jnp.where(((i + ay - j) & (TILE - 1)) == 0, 1.0, 0.0).astype(BF16)
        return [dot(by_rows, dot(f, by_lanes).astype(BF16)) for f in fields]

    for c in loads:
        c.wait()

    @pl.when(d == last)
    def _():
        for slot in (0, 1):
            alive = jnp.where(slot < live_ref[0], 1.0, 0.0).astype(F32)
            for k, f in enumerate(rolled(slot, [exit_v[slot, 0], exit_v[slot, 1]])):
                for h in (0, 1):
                    waves[slot, h, k] = f[h * HALF : (h + 1) * HALF] * alive

    i = lax.broadcasted_iota(jnp.int32, (TILE, TILE), 0)
    j = lax.broadcasted_iota(jnp.int32, (TILE, TILE), 1)
    deal = jnp.where(i == jnp.where(j < HALF, 2 * j, 2 * j - (TILE - 1)), 1.0, 0.0).astype(BF16)
    deal_rows = jnp.where(j == jnp.where(i < HALF, 2 * i, 2 * i - (TILE - 1)), 1.0, 0.0).astype(BF16)
    p = phase[...]
    p0 = p.astype(BF16)
    p1, p2 = halves(p - p0.astype(F32))
    f0, f1, f2 = [dot(deal_rows, dot(q, deal).astype(BF16)) for q in (p0, p1, p2)]
    phase[...] = (f0 + f1) + f2
    for h in (0, 1):
        ordered = phase[part[h], :]
        for k, f in enumerate((jnp.cos(ordered), jnp.sin(ordered))):
            for g in (0, 1):
                rot[k, g, :, part[h]] = f[:, g * HALF : (g + 1) * HALF]

    def roll_incident(slot):
        got = rolled(slot, [inc[li, slot, k] for li in (0, 1) for k in (0, 1)])
        for n, f in enumerate(got):
            inc[n // 2, slot, n % 2] = f.astype(BF16)

    for slot in (0, 1):
        roll_incident(slot)

    zero = jnp.zeros((HALF, HALF), F32)

    def window(li, slot):
        for p, q in quads:
            on_x, on_y = masks(slot, p, q)
            spot = (part[p], part[q])
            for k in (0, 1):
                here = t_own[(li, k) + spot].astype(F32)
                tx, ty, txy = [t_alt[(li, kind, k) + spot].astype(F32) for kind in range(3)]
                t_eff[(li, slot, k) + spot] = jnp.where(
                    on_x, jnp.where(on_y, here, ty), jnp.where(on_y, tx, txy)
                ).astype(BF16)

    def border(li):
        for p in (0, 1):
            edge_x, edge_y = [(n - 1, 0)[p] for n in (n_sx, n_sy)]

            @pl.when(sx == edge_x)
            def _(p=p):
                for kind in (0, 2):
                    t_alt[li, kind, :, part[p], :] = jnp.zeros((2, HALF, TILE), BF16)

            @pl.when(sy == edge_y)
            def _(p=p):
                for kind in (1, 2):
                    t_alt[li, kind, :, :, part[p]] = jnp.zeros((2, TILE, HALF), BF16)

    def windows(li):
        for c in t_copies(li)[1 if li == 1 else 0 :]:
            c.wait_recv()
        border(li)
        for slot in (0, 1):
            window(li, slot)

    def beside(a, b):
        return jnp.concatenate([a, b], axis=1)

    def above(a, b):
        return jnp.concatenate([a, b], axis=0)

    def right(z, first):
        head, tail = halves(z)
        table = jnp.concatenate([m_v[first], m_v[first], m_v[first + 1]], axis=0)
        rows = jnp.concatenate([head, tail, head], axis=1)
        parts = []
        for r in (slice(0, HALF), slice(HALF, 2 * HALF)):
            two = dot(above(head[r], tail[r]), m_v[first])
            parts.append((two[:HALF] + two[HALF:]) + dot(head[r], m_v[first + 1]))
        return above(*parts)

    def left(z, first):
        head, tail = halves(z)
        table = jnp.concatenate([m_v[first], m_v[first + 1], m_v[first]], axis=1)
        cols = jnp.concatenate([head, head, tail], axis=0)
        parts = []
        for r in (slice(0, HALF), slice(HALF, 2 * HALF)):
            two = dot(above(m_v[first, r], m_v[first + 1, r]), head)
            parts.append((two[:HALF] + two[HALF:]) + dot(m_v[first, r], tail))
        return above(*parts)

    c, s = rows_v[0], rows_v[1]

    def between(y):
        a, b = y[:HALF], y[HALF:]
        sm, df = a + b, a - b
        dr, di = df[:, :HALF], df[:, HALF:]
        return above(beside(sm[:, :HALF], dr * c + di * s), beside(sm[:, HALF:], di * c - dr * s))

    def turned(g, x):
        xr, xi = x[:HALF], x[HALF:]
        cp, sp = rot[0, g], rot[1, g]
        return above(xr * cp + xi * sp, xi * cp - xr * sp)

    def undealt(e):
        er, ei = e[:HALF, HALF:], e[HALF:, HALF:]
        tr, ti = er * c - ei * s, ei * c + er * s
        vr, vi = e[:HALF, :HALF], e[HALF:, :HALF]
        return above(beside(vr + tr, vi + ti), beside(vr - tr, vi - ti))

    def finish(joined, store):
        for h in (0, 1):
            e, o = [j[h * HALF : (h + 1) * HALF] for j in joined]
            low, high = e + o, e - o
            store(h, low[:, :HALF], high[:, :HALF], low[:, HALF:], high[:, HALF:])

    def propagated(fields):
        a = [beside(re[:, :HALF], im[:, :HALF]) for re, im in fields]
        b = [beside(re[:, HALF:], im[:, HALF:]) for re, im in fields]
        z0 = above(a[0] + b[0], a[1] + b[1])
        z1 = above(a[0] - b[0], a[1] - b[1])

        y0 = right(z0, 2)
        y1 = right(z1, 6)
        x0 = left(between(y0), 0)
        x1 = left(between(y1), 0)
        e0 = left(turned(0, x0), 2)
        e1 = left(turned(1, x1), 2)
        return [right(undealt(e0), 0), right(undealt(e1), 4)]

    def through(li, slot, h, re, im):
        rows = part[h]
        tr = t_eff[li, slot, 0, rows, :].astype(F32)
        ti = t_eff[li, slot, 1, rows, :].astype(F32)
        return conj_times(tr, ti, re, im)

    def shares(li, slot, p, q):
        wave = waves if li == 1 else middle
        er = inc[li, slot, 0, part[p], part[q]].astype(F32)
        ei = inc[li, slot, 1, part[p], part[q]].astype(F32)
        on_x, on_y = masks(slot, p, q)
        out = []
        for t in conj_times(er, ei, wave[slot, p, 0, :, part[q]], wave[slot, p, 1, :, part[q]]):
            inside = jnp.where(on_x, t, zero)
            beyond = jnp.where(on_x, zero, t)
            out.append(
                [
                    jnp.where(on_y, inside, zero),
                    jnp.where(on_y, beyond, zero),
                    jnp.where(on_y, zero, inside),
                    jnp.where(on_y, zero, beyond),
                ]
            )
        return out

    def first_gradient(li):
        for p, q in quads:
            spot = (part[p], part[q])
            for k, t in enumerate(shares(li, 0, p, q)):
                own[(li, k) + spot] = t[0]
                for kind in range(3):
                    g_alt[(li, kind, k) + spot] = t[kind + 1]

    def second_gradient(li):
        copies = g_copies(li)
        for p, q in quads:
            spot = (part[p], part[q])
            re, im = shares(li, 1, p, q)
            for kind in (2, 0, 1):
                g_out[li, kind, p, q] = coded(
                    g_alt[(li, kind, 0) + spot] + re[kind + 1], g_alt[(li, kind, 1) + spot] + im[kind + 1]
                )
            copies[4 + 2 * p + q].start()
            if q == 1:
                copies[p].start()
            if p == 1:
                copies[2 + q].start()
            own[(li, 0) + spot] += re[0]
            own[(li, 1) + spot] += im[0]

    def gradient(li, slot):
        @pl.when(slot == 0)
        def _():
            first_gradient(li)

        @pl.when(slot == 1)
        def _():
            second_gradient(li)

    def apply_layer(li, slot, source, store):
        fields = [through(li, slot, h, source[slot, h, 0], source[slot, h, 1]) for h in (0, 1)]
        finish(propagated(fields), store)

    @pl.when(odd)
    def _():
        t_copies(1)[0].wait_recv()
        pl.semaphore_signal(go, inc=1, device_id=(d - 1, sx, sy), device_id_type=MESH)

    @pl.when(jnp.logical_not(odd))
    def _():
        pl.semaphore_wait(go, 1)
        share()
        t_copies(1)[0].wait_recv()

    windows(1)

    early = d < 2

    def one_slot(slot, carry):
        @pl.when(d < last)
        def _():
            for h in (0, 1):
                w_copy(slot, h).wait_recv()
                for q in (0, 1):
                    re, im = decoded(words_in[slot, h, q])
                    waves[slot, h, 0, :, part[q]] = re
                    waves[slot, h, 1, :, part[q]] = im

        @pl.when(early)
        def _():
            gradient(1, slot)

        def keep(h, lr, hr, li_, hi_):
            middle[slot, h, 0, :, :HALF] = lr
            middle[slot, h, 0, :, HALF:] = hr
            middle[slot, h, 1, :, :HALF] = li_
            middle[slot, h, 1, :, HALF:] = hi_

        apply_layer(1, slot, waves, keep)

        @pl.when(slot == 0)
        def _():
            windows(0)

        @pl.when(jnp.logical_and(early, slot == 1))
        def _():
            first_gradient(0)
            second_gradient(0)

        @pl.when(d > 0)
        def _():
            def encode(h, lr, hr, li_, hi_):
                words_out[slot, h, 0] = coded(lr, li_)
                words_out[slot, h, 1] = coded(hr, hi_)
                w_copy(slot, h).start()

            apply_layer(0, slot, middle, encode)

        return carry

    lax.fori_loop(0, 2, one_slot, 0)

    @pl.when(jnp.logical_not(early))
    def _():
        for li in (1, 0):
            first_gradient(li)
            second_gradient(li)

    for li in (1, 0):
        for c in t_copies(li):
            c.wait_send()

    @pl.when(d > 0)
    def _():
        for slot in (0, 1):
            for h in (0, 1):
                w_copy(slot, h).wait_send()

    from_x = [jnp.where(sx > 0, 1.0, 0.0), jnp.where(sx < n_sx - 1, 1.0, 0.0)]
    from_y = [jnp.where(sy > 0, 1.0, 0.0), jnp.where(sy < n_sy - 1, 1.0, 0.0)]
    for li in (1, 0):
        copies = g_copies(li)
        for p, q in quads:
            if q == 0:
                copies[p].wait_recv()
            if p == 0:
                copies[2 + q].wait_recv()
            copies[4 + 2 * p + q].wait_recv()
            weights = (from_x[p], from_y[q], from_x[p] * from_y[q])
            got = [decoded(g_in[li, kind, p, q], weights[kind] / 32767.0) for kind in range(3)]
            for k in (0, 1):
                own[li, k, part[p], part[q]] += (got[0][k] + got[1][k]) + got[2][k]

    for li in (1, 0):
        for c in g_copies(li):
            c.wait_send()


def shards(transmission, incident, exit_adjoint, propagator_phase, scan_anchor, live_count):
    sizes = tuple(lax.axis_size(a) for a in ("depth", "sx", "sy"))
    slab = transmission.shape[0]
    any_space = pl.BlockSpec(memory_space=pl.ANY)
    plane = (TILE, TILE)
    dma = pltpu.SemaphoreType.DMA
    return pl.pallas_call(
        functools.partial(kernel, sizes),
        out_shape=pltpu.VMEM(transmission.shape, F32),
        in_specs=[any_space] * 8,
        out_specs=pl.BlockSpec(memory_space=pltpu.VMEM),
        scratch_shapes=[
            pltpu.VMEM((slab, 2) + plane, BF16),
            pltpu.VMEM((slab, 3, 2) + plane, BF16),
            pltpu.VMEM((slab, 2, 2) + plane, BF16),
            pltpu.VMEM((slab, 2, 2) + plane, BF16),
            pltpu.VMEM((2, 2) + plane, BF16),
            pltpu.VMEM(plane, F32),
            pltpu.VMEM((2, 2, HALF, TILE), F32),
            pltpu.VMEM((8,) + plane, BF16),
            pltpu.VMEM((2, HALF, HALF), F32),
            pltpu.VMEM((2, 2, 2, HALF, TILE), F32),
            pltpu.VMEM((2, 2, 2, HALF, TILE), F32),
            pltpu.VMEM((2, 2, 2, CODED, HALF), jnp.int32),
            pltpu.VMEM((2, 2, 2, CODED, HALF), jnp.int32),
            pltpu.VMEM((slab, 3, 2) + plane, F32),
            pltpu.VMEM((slab, 3, 2, 2, CODED, HALF), jnp.int32),
            pltpu.VMEM((slab, 3, 2, 2, CODED, HALF), jnp.int32),
            dma((8,)),
            dma((16,)),
            dma((16,)),
            dma((4,)),
            dma((4,)),
            dma((16,)),
            dma((16,)),
            pltpu.SemaphoreType.REGULAR,
            pltpu.SMEM((2, 2), jnp.int32),
            pltpu.SMEM((1,), jnp.int32),
        ],
        compiler_params=pltpu.CompilerParams(
            collective_id=0, has_side_effects=True, vmem_limit_bytes=60 * 1024 * 1024
        ),
    )(
        transmission,
        incident,
        exit_adjoint,
        propagator_phase,
        jnp.asarray(dft_tables()),
        jnp.asarray(row_twiddles()),
        scan_anchor,
        live_count,
    )


def solution(mesh):
    placed = (
        P("depth", None, "sx", "sy"),
        P("depth", ("sx", "sy"), None, None, None),
        P(("sx", "sy"), None, None, None),
        P(),
        P(("sx", "sy"), None),
        P(("sx", "sy")),
    )
    return jax.shard_map(
        shards, mesh=mesh, in_specs=placed, out_specs=P("depth", None, "sx", "sy"), check_vma=False
    )
```
